256 devices in a mesh: tile: 64 (over z, y_lo, x), lev: 4 (over y_hi, core).
Axes of the slice: x: 4, y: 4 (y_hi: 2, y_lo: 2; y = y_hi * 2 + y_lo), z: 8, core: 2. Of those that a mesh axis runs over, the one named last changes fastest.
Arguments:
- control_static: float32 [2, 128, 512, 128], P(None, 'lev', 'tile'), may hold values from -6 to 6
- control_ens: float32 [2, 128, 512, 128], P(None, 'lev', 'tile'), may hold values from -6 to 6
- ens_perts: bfloat16 [2, 2, 128, 512, 128], P(None, None, 'lev', 'tile'), may hold values from -2.5 to 2.5
- band_sqrt: float32 [64, 2, 128, 128], P('tile', None, 'lev'), may hold values from -1 to 2
- band_owner: int32 [64], replicated, may hold values from 0 to 63, each once
- scale_class: int32 [512, 128], P('tile'), may hold values from 0 to 7
- static_scales: float32 [8], replicated, may hold values from 0.5 to 4
- local_scales: float32 [8], replicated, may hold values from 1 to 8
- obs_source: int32 [32768, 1], P('tile'), may hold values from 0 to 63; in each aligned block of 512 rows (0 to 511, 512 to 1023, ...) at most 32 rows name the same one
- obs_column: int32 [32768], P('tile'), may hold values from 0 to 1023
- obs_jac: float32 [64, 128, 2, 128], P('tile', None, None, 'lev'), may hold values from -0.375 to 0.375
- innovation: float32 [128, 32768], P(None, 'tile'), may hold values from -6 to 6
- obs_weight: float32 [128, 32768], P(None, 'tile'), may hold values from 0.2 to 5
Outputs:
- analysis_increment: float32 [2, 128, 512, 128], P(None, 'lev', 'tile')
- final_static: float32 [2, 128, 512, 128], P(None, 'lev', 'tile')
- final_ens: float32 [2, 128, 512, 128], P(None, 'lev', 'tile')
The draws below stay inside these ranges and needn't reach their ends.
Inputs may be any that keep to these rules, and one draw needn't show every extreme that they name: `obs_source`: within each tile's block of 512 observations at most 32 name the same source tile, and some source tile is named exactly 32 times in some block. `band_owner`: each slot is named once.
All inputs are finite; a program needn't handle non-finite values.
Results may differ from the reference program's by a relative error of at most 0.0003.
Values sent between devices are 32-bit elements; how exact they have to be, the bound alone decides.
No kernel may reach another device: no remote copies, remote signals or barrier semaphores. Data moves between devices by JAX's collectives and lax.ppermute only.
A program may use at most 64 MiB of HBM per device.

```python
import math
import jax
import jax.numpy as jnp
import numpy as np
from jax import lax

NVAR = 2
NLEV = 128
NCH = 128
NCLS = 8
NSWEEP = 4
ITERS = 2
LON_DEV = 8
LAT = 128
OBS_DEV = 512
ENS = 2
NLON = 512
NBAND = 64
CAP = 32
NOBS = 32768
N_TILE = 64


def draw_band_sqrt(key, part):
    first_key = jax.random.fold_in(key, 11)
    second_key = jax.random.fold_in(key, 23)
    shape_full = (NBAND, NVAR, NLEV, NLEV)
    spread_part = jnp.clip(jax.random.normal(first_key, shape_full, jnp.float32), -4.0, 4.0)
    off_diagonal = spread_part * (0.5 / math.sqrt(NLEV))
    diagonal = jax.random.uniform(second_key, (NBAND, NVAR, NLEV), jnp.float32, 0.6, 1.4)
    identity = (lax.broadcasted_iota(jnp.int32, (NLEV, NLEV), 0) == lax.broadcasted_iota(jnp.int32, (NLEV, NLEV), 1)).astype(jnp.float32)
    return off_diagonal + diagonal[..., None] * identity


def place_ends(values, key, least, high):
    place = [jax.random.randint(jax.random.fold_in(key, axis), (), 0, length) for axis, length in enumerate(values.shape)]
    main_axis = values.shape.index(max(values.shape))
    neighbour = place[:main_axis] + [(place[main_axis] + 1) % values.shape[main_axis]] + place[main_axis + 1:]
    return values.at[tuple(place)].set(least).at[tuple(neighbour)].set(high)


def level_of(stream_key, shape, pieces, smallest, high):
    level, own = 1.0, jax.random.fold_in(stream_key, 6)
    for position, shards_of in pieces:
        draws = jnp.exp(jax.random.uniform(jax.random.fold_in(own, position), (shards_of,), jnp.float32, smallest / len(pieces), high / len(pieces)))
        level = level * jnp.repeat(draws, shape[position] // shards_of).reshape([-1 if axis == position else 1 for axis in range(len(shape))])
    return level


def shared_out(key, own, number, rows, amount, top, bound, skew):
    sequence = jax.random.permutation(key, amount)
    heavy_load, ordinary = load_shares(amount, rows * top, bound, skew, True), load_shares(amount, rows * top, bound, skew, False)
    places = jnp.arange(amount)

    def named(tallies, rotation):
        used = int((tallies > 0).sum())
        fixed = max(1, used // 4)
        passed = fixed + (places - fixed + rotation * (used - fixed)) % max(1, amount - fixed)
        return jnp.zeros((amount,), jnp.int32).at[sequence[jnp.where(places < fixed, places, passed)]].set(jnp.asarray(tallies, jnp.int32))

    tallies = jnp.where(number % 4 == 0, named(heavy_load, number // 4), named(ordinary, number - number // 4 - 1))
    mixed = jax.random.permutation(jax.random.fold_in(own, 3), amount)
    source_of, sink = mixed[0:amount // 2 * 2:2], mixed[1:amount // 2 * 2:2]
    room = jnp.minimum(tallies[source_of] - 1, bound - tallies[sink]) // 2
    room = jnp.where((source_of == sequence[0]) | (sink == sequence[0]) | (tallies[sink] == 0), 0, jnp.maximum(room, 0))
    passed = jax.random.randint(jax.random.fold_in(own, 4), (amount // 2,), 0, 1 << 20) % (room + 1)
    tallies = tallies.at[source_of].add(-passed).at[sink].add(passed)
    labels = jnp.searchsorted(jnp.cumsum(tallies), jnp.arange(rows * top), side="right").astype(jnp.int32)
    table = labels.reshape(top, rows).T
    table = table[jax.random.permutation(jax.random.fold_in(own, 1), rows)]
    rotation = jax.random.randint(jax.random.fold_in(own, 2), (rows, 1), 0, top)
    return jnp.take_along_axis(table, (jnp.arange(top)[None, :] + rotation) % top, axis=1)


def load_shares(count, total, limit, slope, full):
    weights = [(1 << 20) // math.isqrt(standing ** slope) + 1 for standing in range(1, count + 1)]
    largest = limit if full else min(limit, max(-(-total // count), total * weights[0] // sum(weights)))
    least = 1 if total - largest >= count - 1 else 0
    holding, surplus = [largest] + [least] * (count - 1), total - largest - least * (count - 1)
    while surplus > 0:
        candidates = [i for i in range(1, count) if holding[i] < largest] or [i for i in range(1, count) if holding[i] < limit]
        mass, budget = sum([weights[i] for i in candidates]), surplus
        for i in candidates:
            addition = min(limit - holding[i], max(1, budget * weights[i] // mass), surplus)
            holding[i] = holding[i] + addition
            surplus = surplus - addition
    return np.array(holding)


def gaussian(stream_key, dims, scale, limit, split=(), kind=jnp.bfloat16):
    gain = level_of(stream_key, dims, split, -0.22, 0.18) if split else 1.0
    drawn = jax.random.normal(stream_key, dims, jnp.float32) * scale * gain
    return jnp.minimum(jnp.maximum(drawn, -limit), limit).astype(kind)


def setup_inputs(seed: int = 0) -> dict:
    keys = jax.random.split(jax.random.key(seed), 14)
    control_static = gaussian(keys[0], (NVAR, NLEV, NLON, LAT), 1.0, 6.0, ((1, 4), (2, 64)), jnp.float32)
    control_ens = gaussian(keys[1], (ENS, NLEV, NLON, LAT), 1.0, 6.0, ((1, 4), (2, 64)), jnp.float32)
    ens_perts = gaussian(keys[2], (ENS, NVAR, NLEV, NLON, LAT), 0.35, 2.5, ((2, 4), (3, 64)))
    band_sqrt = draw_band_sqrt(jax.random.fold_in(keys[13], 71), 0)
    band_owner = jax.random.permutation(keys[4], NBAND).astype(jnp.int32)
    scale_class = place_ends(jax.random.randint(keys[5], (NLON, LAT), 0, NCLS), jax.random.fold_in(keys[5], 1), 0, NCLS - 1).astype(jnp.int32)
    static_scales = jnp.clip(jnp.exp(jax.random.uniform(keys[6], (NCLS,), jnp.float32, math.log(0.5), math.log(4.0))), 0.5, 4.0)
    local_scales = jnp.clip(jnp.exp(jax.random.uniform(keys[7], (NCLS,), jnp.float32, math.log(1.0), math.log(8.0))), 1.0, 8.0)
    obs_source_keys = jax.random.split(jax.random.fold_in(keys[8], 1), NOBS // OBS_DEV)
    obs_source_turns = jax.random.permutation(jax.random.fold_in(keys[8], 3), NOBS // OBS_DEV)
    obs_source = jax.vmap(lambda own, number: shared_out(jax.random.fold_in(keys[8], 2), own, number, OBS_DEV, N_TILE, 1, CAP, 2))(obs_source_keys, obs_source_turns).reshape((NOBS, 1))
    obs_column = place_ends(jax.random.randint(keys[9], (NOBS,), 0, LON_DEV * LAT), jax.random.fold_in(keys[9], 1), 0, (LON_DEV * LAT) - 1).astype(jnp.int32)
    obs_jac = gaussian(keys[10], (N_TILE, NCH, NVAR, NLEV), (NVAR * NLEV) ** -0.5, 0.375, ((0, 64), (3, 4)), jnp.float32)
    innovation = gaussian(keys[11], (NCH, NOBS), 1.0, 6.0, ((1, 64),), jnp.float32)
    obs_weight = jnp.clip(jnp.exp(math.log(5.0) - 3.218876 * jax.random.uniform(keys[12], (NCH, NOBS), jnp.float32) ** level_of(keys[12], (NCH, NOBS), ((1, 64),), -0.2, 0.2)), 0.2, 5.0)
    return {"control_static": control_static, "control_ens": control_ens, "ens_perts": ens_perts, "band_sqrt": band_sqrt, "band_owner": band_owner, "scale_class": scale_class, "static_scales": static_scales, "local_scales": local_scales, "obs_source": obs_source, "obs_column": obs_column, "obs_jac": obs_jac, "innovation": innovation, "obs_weight": obs_weight}


beta_static = 0.8
beta_ensemble = 0.6
step_length = 0.3
highest = lax.Precision.HIGHEST

def face_weights(kappas):
    eastward = 0.5 * (kappas + jnp.roll(kappas, -1, axis=1))
    westward = jnp.roll(eastward, 1, axis=1)
    interior = 0.5 * (kappas[:, :, :-1] + kappas[:, :, 1:])
    edge_zero = jnp.zeros(kappas.shape[:2] + (1,), jnp.float32)
    northward = jnp.concatenate([interior, edge_zero], axis=2)
    southward = jnp.concatenate([edge_zero, interior], axis=2)
    inverse_diag = 1.0 / (1.0 + eastward + westward + northward + southward)
    return (eastward, westward, northward, southward, inverse_diag)

def per_row(weights, static_rows, member_rows):

    def spread_rows(kind_field):
        first = jnp.broadcast_to(kind_field[0:1], (static_rows,) + kind_field.shape[1:])
        second = jnp.broadcast_to(kind_field[1:2], (member_rows,) + kind_field.shape[1:])
        return jnp.concatenate([first, second], axis=0)[:, None]
    return tuple((spread_rows(kind_field) for kind_field in weights))

def lateral(state_field, weights):
    edge_zero = jnp.zeros(state_field.shape[:-1] + (1,), jnp.float32)
    upward = jnp.concatenate([state_field[..., 1:], edge_zero], axis=-1)
    downward = jnp.concatenate([edge_zero, state_field[..., :-1]], axis=-1)
    return weights[2] * upward + weights[3] * downward

def neighbours(state_field, weights):
    return weights[0] * jnp.roll(state_field, -1, axis=2) + weights[1] * jnp.roll(state_field, 1, axis=2) + lateral(state_field, weights)

def diffuse(source_field, weights):
    current = source_field
    for sweep_index in range(NSWEEP):
        current = weights[4] * (source_field + neighbours(current, weights))
    return current

def vertical(state_field, matrices):
    shaped = state_field.reshape(NVAR, NLEV, NLON, NBAND, LAT // NBAND)
    mixed_rows = jnp.einsum('bvlm,vmxbr->vlxbr', matrices, shaped, precision=highest)
    return mixed_rows.reshape(NVAR, NLEV, NLON, LAT)

def reference(control_static, control_ens, ens_perts, band_sqrt, band_owner, scale_class, static_scales, local_scales, obs_source, obs_column, obs_jac, innovation, obs_weight):
    kappas = jnp.stack([static_scales[scale_class], local_scales[scale_class]])
    weights = per_row(face_weights(kappas), NVAR, ENS)
    matrices = band_sqrt[band_owner]
    members = ens_perts.astype(jnp.float32)
    columns_global = (obs_source[:, 0] * (LON_DEV * LAT) + obs_column).astype(jnp.int32)
    jacobian = obs_jac.reshape(N_TILE, NCH, NVAR * NLEV)

    def increment(static_part, ensemble_part):
        stacked = jnp.concatenate([vertical(static_part, matrices), ensemble_part], axis=0)
        smoothed = diffuse(stacked, weights)
        return beta_static * smoothed[:NVAR] + beta_ensemble * lax.optimization_barrier(jnp.sum(members * smoothed[NVAR:, None], axis=0))

    def misfit(static_part, ensemble_part):
        state = increment(static_part, ensemble_part)
        flattened = state.reshape(NVAR * NLEV, NLON * LAT)
        picked = jnp.take(flattened, columns_global, axis=1).reshape(NVAR * NLEV, N_TILE, OBS_DEV)
        observed = jnp.einsum('tcj,jto->cto', jacobian, picked, precision=highest).reshape(NCH, N_TILE * OBS_DEV)
        departure = observed - innovation
        control_term = jnp.sum(static_part * static_part) + jnp.sum(ensemble_part * ensemble_part)
        return 0.5 * control_term + 0.5 * jnp.sum(obs_weight * departure * departure)
    gradient = jax.grad(misfit, argnums=(0, 1))
    static_part = control_static
    ensemble_part = control_ens
    for iteration in range(ITERS):
        grad_static, grad_ensemble = gradient(static_part, ensemble_part)
        static_part = static_part - step_length * grad_static
        ensemble_part = ensemble_part - step_length * grad_ensemble
    return (increment(static_part, ensemble_part), static_part, ensemble_part)
```

```python
import functools

import jax
import jax.numpy as jnp
from jax import lax
from jax.experimental import pallas as pl
from jax.experimental.pallas import tpu as pltpu
from jax.sharding import Mesh, PartitionSpec as P

NSWEEP = 4
ITERS = 2

beta_static = 0.8
beta_ensemble = 0.6
step_length = 0.3

LEV = ("yh", "core")
TILE = ("z", "yl", "x")
PLANE = ("yl", "x", "yh", "core")
ALL = ("z", "yl", "x", "yh", "core")

f32, bf16, i32 = jnp.float32, jnp.bfloat16, jnp.int32


def iota(shape, dim):
    return lax.broadcasted_iota(i32, shape, dim)


def split(value):
    high = value.astype(bf16)
    return high, (value - high.astype(f32)).astype(bf16)


def dot_nn(a, b):
    return lax.dot_general(a, b, (((1,), (0,)), ((), ())), preferred_element_type=f32)


def dot_nt(a, b):
    return lax.dot_general(a, b, (((1,), (1,)), ((), ())), preferred_element_type=f32)


def dot_tn(a, b):
    return lax.dot_general(a, b, (((0,), (0,)), ((), ())), preferred_element_type=f32)


def three(dot, a, b):
    (ah, al), (bh, bl) = split(a), split(b)
    return dot(ah, bh) + (dot(ah, bl) + dot(al, bh))


def one_hot(mask):
    return jnp.where(mask, 1.0, 0.0).astype(bf16)


def call(kernel, outs, scratch=(), smem=0, total=0, flops=10**8, size=2 * 10**6):
    spaces = [pl.BlockSpec(memory_space=pltpu.SMEM)] * smem
    spaces += [pl.BlockSpec(memory_space=pltpu.VMEM)] * (total - smem)
    return pl.pallas_call(
        kernel,
        out_shape=[jax.ShapeDtypeStruct(shape, kind) for shape, kind in outs],
        in_specs=spaces,
        out_specs=[pl.BlockSpec(memory_space=pltpu.VMEM)] * len(outs),
        scratch_shapes=[pltpu.VMEM(shape, kind) for shape, kind in scratch],
        compiler_params=pltpu.CompilerParams(vmem_limit_bytes=40 * 2**20),
        cost_estimate=pl.CostEstimate(flops=flops, bytes_accessed=size, transcendentals=0),
    )


def selector(owner):
    row, lane = iota((512, 128), 0), iota((512, 128), 1)
    slot = (((row >> 4) & 3) * 2 + ((row >> 1) & 1)) * 8 + (row >> 6)
    hit = (owner == slot) & ((lane & 1) == (row & 1))
    pair = (row >> 2) & 3
    return jnp.concatenate([one_hot(hit & (pair == q)) for q in range(4)], axis=1)


def pack(field, owner):
    wide = jnp.concatenate([field(q) for q in range(4)], axis=1)
    high, low = split(wide)
    chosen = selector(owner)
    return dot_nt(chosen, high) + dot_nt(chosen, low)


def unpack(rows, owner):
    high, low = split(rows)
    chosen = selector(owner)
    return dot_tn(high, chosen) + dot_tn(low, chosen)


def begin_kernel(owner, static_in, ens_in, perts_in, classes, packed, up, down, ens, perts, work, flat):
    for lon in range(8):
        work[lon] = static_in[pl.ds(lon, 64, stride=8), :]
    packed[...] = pack(lambda q: work[2 * q : 2 * q + 2].reshape(128, 128), owner[...])
    flat[...] = perts_in[...].astype(f32).reshape(1024, 128)
    for lon in range(8):
        member = ens_in[pl.ds(lon, 64, stride=8), :]
        weight = flat[pl.ds(lon, 128, stride=8), :]
        ens[lon] = member
        perts[lon] = weight
        target, place = (down, lon) if lon < 4 else (up, lon - 4)
        target[place * 64 : place * 64 + 64] = member
        target[256 + place * 128 : 384 + place * 128] = weight
    marks = classes[...].astype(f32)
    up[768:776] = marks
    down[768:776] = marks


def request_kernel(here, source_row, source_col, column_row, weight, innovation, request, weights, targets):
    level = here[1]
    later = iota((512, 512), 0) < iota((512, 512), 1)
    same = (source_col[...] == source_row[...]) & later
    rank = jnp.sum(jnp.where(same, 1.0, 0.0), axis=0, keepdims=True).astype(i32)
    source = source_row[...]
    wanted = column_row[...] + 1
    from_tile = iota((64, 512), 0) == source
    ranked = one_hot(iota((128, 512), 0) == rank)
    high = jnp.where(from_tile, (wanted >> 5).astype(f32), 0.0).astype(bf16)
    low = jnp.where(from_tile, (wanted & 31).astype(f32), 0.0).astype(bf16)
    request[...] = (32.0 * dot_nt(high, ranked) + dot_nt(low, ranked)).astype(i32)
    row = iota((256, 512), 0)
    weight_terms, innovation_terms = split(weight[...]), split(innovation[...])
    for half in range(2):
        place = level * 8 + (row >> 6) * 2 + half
        mine = one_hot(((row & 63) == source) & (rank == place))
        lanes = slice(half * 128, half * 128 + 128)
        weights[:, lanes] = dot_nt(mine, weight_terms[0]) + dot_nt(mine, weight_terms[1])
        targets[:, lanes] = dot_nt(mine, innovation_terms[0]) + dot_nt(mine, innovation_terms[1])


def load_matrices(here, first, second, matrices):
    z = here[0]
    for j, part in enumerate((first, second)):
        half = lax.rem(z + j, 2)
        for k in range(4):
            block = lax.rem(lax.div(z, 2) + 4 - k, 4)
            rows = pl.ds(pl.multiple_of(block * 32, 32), 32)
            for var in range(2):
                start = k * 64 + var * 32
                matrices[half * 2 + var, rows, :] = part[start : start + 32]


def columns_of(rows):
    blocks = [
        jnp.concatenate([rows[u * 64 + l * 16 : u * 64 + l * 16 + 16] for u in range(8)], axis=0)
        for l in range(4)
    ]
    chunk = iota((128, 128), 1) >> 5
    out = []
    for c in range(4):
        joined = None
        for l in range(4):
            shift = (32 * (l - c)) % 128
            moved = pltpu.roll(blocks[l], shift, 1) if shift else blocks[l]
            joined = moved if l == 0 else jnp.where(chunk == l, moved, joined)
        out.append(joined)
    return out


def store_columns(out, columns, stride, offset):
    chunk = iota((128, 128), 1) >> 5
    for l in range(4):
        joined = None
        for c in range(4):
            shift = (32 * (c - l)) % 128
            moved = pltpu.roll(columns[c], shift, 1) if shift else columns[c]
            joined = moved if c == 0 else jnp.where(chunk == c, moved, joined)
        for u in range(8):
            start = (u * 4 + l) * stride + offset
            out[start : start + 16] = joined[u * 16 : u * 16 + 16]


def choose_half(product):
    half = (iota((256, 128), 0) >> 1) & 1
    return jnp.where(half == 0, product[:, :128], product[:, 128:])


def forward_columns(columns, matrices):
    out = [None] * 4
    for var in range(2):
        stacked = jnp.concatenate([columns[var], columns[2 + var]], axis=0)
        pair = jnp.concatenate([matrices[var], matrices[2 + var]], axis=0)
        chosen = choose_half(three(dot_nt, stacked, pair))
        out[var], out[2 + var] = chosen[:128], chosen[128:]
    return out


def backward_columns(columns, matrices):
    out = [None] * 4
    for var in range(2):
        stacked = jnp.concatenate([columns[var], columns[2 + var]], axis=0)
        pair = jnp.concatenate([matrices[var], matrices[2 + var]], axis=1)
        chosen = choose_half(three(dot_nn, stacked, pair))
        out[var], out[2 + var] = chosen[:128], chosen[128:]
    return out


def first_columns_kernel(here, rows, first, second, state, out, matrices):
    load_matrices(here, first, second, matrices)
    columns = columns_of(rows[...])
    for c in range(4):
        state[c] = columns[c]
    store_columns(out, forward_columns(columns, matrices), 16, 0)


def columns_kernel(last, here, rows, first, second, state, *refs):
    out, matrices = refs[-2], refs[-1]
    load_matrices(here, first, second, matrices)
    pulled = backward_columns(columns_of(rows[...]), matrices)
    columns = [(1.0 - step_length) * state[c] - step_length * pulled[c] for c in range(4)]
    forward = forward_columns(columns, matrices)
    if last:
        store_columns(out, forward, 32, 0)
        store_columns(out, columns, 32, 16)
    else:
        for c in range(4):
            refs[0][c] = columns[c]
        store_columns(out, forward, 16, 0)


def edges_kernel(owner, rows, low, high):
    wide = unpack(rows[...], owner[...])
    for lon in range(8):
        target, place = (low, lon) if lon < 4 else (high, lon - 4)
        q, side = lon // 2, lon % 2
        target[place] = wide[side * 64 : side * 64 + 64, q * 128 : q * 128 + 128]


def last_edges_kernel(owner, rows, low, high, final_static):
    both = rows[...]
    for kind in range(2):
        part = jnp.concatenate([both[p * 32 + kind * 16 : p * 32 + kind * 16 + 16] for p in range(32)], axis=0)
        wide = unpack(part, owner[...])
        for lon in range(8):
            q, side = lon // 2, lon % 2
            value = wide[side * 64 : side * 64 + 64, q * 128 : q * 128 + 128]
            if kind == 0:
                target, place = (low, lon) if lon < 4 else (high, lon - 4)
                target[place] = value
            else:
                final_static[pl.ds(lon, 64, stride=8), :] = value


def face_weights(scales, before, own, after, kappa, weights):
    marks = jnp.concatenate([before, own, after], axis=0)
    lane = iota((16, 128), 1)
    for kind in range(2):
        value = jnp.zeros((24, 128), f32)
        for entry in range(8):
            value = jnp.where(marks == float(entry), scales[kind * 8 + entry], value)
        kappa[kind] = value
        centre = kappa[kind, 4:20]
        east = 0.5 * (centre + kappa[kind, 5:21])
        west = 0.5 * (kappa[kind, 3:19] + centre)
        north = jnp.where(lane < 127, 0.5 * (centre + pltpu.roll(centre, 127, 1)), 0.0)
        south = jnp.where(lane > 0, 0.5 * (centre + pltpu.roll(centre, 1, 1)), 0.0)
        weights[kind, 0] = east
        weights[kind, 1] = west
        weights[kind, 2] = north
        weights[kind, 3] = south
        weights[kind, 4] = 1.0 / (1.0 + east + west + north + south)


def neighbours(field, i, weight):
    return (
        weight(0, i) * field[i + 1]
        + weight(1, i) * field[i - 1]
        + weight(2, i) * pltpu.roll(field[i], 127, 1)
        + weight(3, i) * pltpu.roll(field[i], 1, 1)
    )


def diffuse(source, weight):
    current = dict(enumerate(source))
    for sweep in range(NSWEEP):
        current = {
            i: weight(4, i) * (source[i] + neighbours(current, i, weight))
            for i in range(sweep + 1, 15 - sweep)
        }
    return current


def diffuse_transposed(source, weight):
    carried = dict(enumerate(source))
    total = None
    for sweep in range(NSWEEP):
        scaled = {i: weight(4, i) * carried[i] for i in range(sweep, 16 - sweep)}
        total = {i: scaled[i] if total is None else total[i] + scaled[i] for i in range(4, 12)}
        carried = {i: neighbours(scaled, i, weight) for i in range(sweep + 1, 15 - sweep)}
    return {i: total[i] + carried[i] for i in range(4, 12)}


def weight_of(weights, kind):
    return lambda which, i: weights[kind, which, i : i + 1, :]


def wide_loader(before, low, high, after):
    parts = (before, low, high, after)
    return lambda rows: [parts[i // 4][i % 4, rows, :] for i in range(16)]


def increments(loader, ens, ens_before, ens_after, perts, weights, target):

    def ens_at(rows):
        return (
            [ens_before[pl.ds(i * 64 + rows, 8), :] for i in range(4)]
            + [ens[i, pl.ds(rows, 8), :] for i in range(8)]
            + [ens_after[pl.ds(i * 64 + rows, 8), :] for i in range(4)]
        )

    def levels(step, carry):
        base = pl.multiple_of(step * 8, 8)
        members = [diffuse(ens_at(e * 32 + base), weight_of(weights, 1)) for e in range(2)]
        for var in range(2):
            smooth = diffuse(loader(pl.ds(var * 32 + base, 8)), weight_of(weights, 0))
            for lon in range(8):
                total = sum(
                    perts[lon, pl.ds((e * 2 + var) * 32 + base, 8), :] * members[e][lon + 4] for e in range(2)
                )
                target[lon, pl.ds(var * 32 + base, 8), :] = (
                    beta_static * smooth[lon + 4] + beta_ensemble * total
                )
        return carry

    lax.fori_loop(0, 4, levels, 0)


def slot_columns(request):
    wanted = request[...]
    repeat = one_hot((iota((1024, 64), 0) >> 4) == iota((1024, 64), 1))
    high = (wanted >> 5).astype(f32).astype(bf16)
    low = (wanted & 31).astype(f32).astype(bf16)
    spread = 32.0 * dot_nn(repeat, high) + dot_nn(repeat, low)
    lane, place = iota((1024, 128), 1), (iota((1024, 128), 0) & 15) * 2
    return [
        jnp.sum(jnp.where(lane == place + half, spread, 0.0), axis=1, keepdims=True).astype(i32) - 1
        for half in range(2)
    ]


def observe_kernel(
    scales, request, low, high, before, after, ens, ens_before, ens_after, perts, marks_before, own_marks, marks_after,
    out, kappa, weights, field,
):
    face_weights(scales, marks_before[...], own_marks[...].astype(f32), marks_after[...], kappa, weights)
    increments(wide_loader(before, low, high, after), ens, ens_before, ens_after, perts, weights, field)
    places = slot_columns(request)
    lane = iota((1024, 256), 1)
    sums = [None, None]
    for q in range(4):
        pair = jnp.concatenate([field[2 * q], field[2 * q + 1]], axis=1)
        terms = jnp.concatenate(split(pair), axis=0)
        for half in range(2):
            part = dot_nt(one_hot(places[half] - q * 256 == lane), terms)
            sums[half] = part if sums[half] is None else sums[half] + part
    folded = [value + pltpu.roll(value, 64, 1) for value in sums]
    out[...] = jnp.where(iota((1024, 128), 1) < 64, folded[0], folded[1])


def last_kernel(
    scales, low, high, before, after, ens, ens_before, ens_after, perts, marks_before, own_marks, marks_after,
    out, final_ens, kappa, weights, field,
):
    face_weights(scales, marks_before[...], own_marks[...].astype(f32), marks_after[...], kappa, weights)
    increments(wide_loader(before, low, high, after), ens, ens_before, ens_after, perts, weights, field)
    for lon in range(8):
        out[pl.ds(lon, 64, stride=8), :] = field[lon]
        final_ens[pl.ds(lon, 64, stride=8), :] = ens[lon]


def operators_kernel(here, arrived, own, near, middle, far, weights, targets, out, operators):
    level = here[1]
    lane = iota((64, 128), 1)
    for k, part in enumerate((own, near, middle, far)):
        block = lax.rem(level + 4 - k, 4)
        value = part[...]
        moved = pltpu.roll(value, 64, 1)
        operators[block, 0:64] = jnp.where(lane < 64, value, 0.0)
        operators[block, 64:128] = jnp.where(lane < 64, moved, 0.0)
        operators[block, 128:192] = jnp.where(lane < 64, 0.0, moved)
        operators[block, 192:256] = jnp.where(lane < 64, 0.0, value)
    observed = None
    for l in range(4):
        rows = jnp.concatenate([arrived[pl.ds(l * 4 + j, 64, stride=16), :] for j in range(4)], axis=0)
        part = three(dot_nt, rows, operators[l])
        observed = part if observed is None else observed + part
    departure = weights[...] * (observed - targets[...])
    for l in range(4):
        pulled = three(dot_nn, departure, operators[l])
        for j in range(4):
            out[pl.ds(l * 4 + j, 64, stride=16), :] = pulled[j * 64 : j * 64 + 64]


def collect_kernel(request, arrived, low, high):
    places = slot_columns(request)
    value = arrived[...]
    first = value.astype(bf16).astype(f32)
    rest = value - first
    lane = iota((1024, 128), 1) < 64
    stacked = jnp.concatenate(
        [
            jnp.where(lane, first, pltpu.roll(rest, 64, 1)),
            jnp.where(lane, pltpu.roll(first, 64, 1), rest),
        ],
        axis=0,
    ).astype(bf16)
    wide_lane = iota((1024, 256), 1)
    for q in range(4):
        hits = jnp.concatenate([one_hot(places[half] - q * 256 == wide_lane) for half in range(2)], axis=0)
        both = dot_tn(stacked, hits)
        total = both[:64] + both[64:]
        target = low if q < 2 else high
        for side in range(2):
            target[(q % 2) * 2 + side] = total[:, side * 128 : side * 128 + 128]


def pull_kernel(
    scales, owner, low, high, before, after, ens, perts, perts_before, perts_after, marks_before, own_marks, marks_after,
    packed, new_ens, new_low, new_high, kappa, weights, field,
):
    face_weights(scales, marks_before[...], own_marks[...].astype(f32), marks_after[...], kappa, weights)
    loader = wide_loader(before, low, high, after)

    def perts_at(rows):
        return (
            [perts_before[pl.ds(i * 128 + rows, 8), :] for i in range(4)]
            + [perts[i, pl.ds(rows, 8), :] for i in range(8)]
            + [perts_after[pl.ds(i * 128 + rows, 8), :] for i in range(4)]
        )

    def levels(step, carry):
        base = pl.multiple_of(step * 8, 8)
        gradient = [loader(pl.ds(var * 32 + base, 8)) for var in range(2)]
        for var in range(2):
            smooth = diffuse_transposed([beta_static * value for value in gradient[var]], weight_of(weights, 0))
            for lon in range(8):
                field[lon, pl.ds(var * 32 + base, 8), :] = smooth[lon + 4]
        for e in range(2):
            factors = [perts_at((e * 2 + var) * 32 + base) for var in range(2)]
            mixed = [
                beta_ensemble * (factors[0][i] * gradient[0][i] + factors[1][i] * gradient[1][i]) for i in range(16)
            ]
            smooth = diffuse_transposed(mixed, weight_of(weights, 1))
            rows = pl.ds(e * 32 + base, 8)
            for lon in range(8):
                value = (1.0 - step_length) * ens[lon, rows, :] - step_length * smooth[lon + 4]
                new_ens[lon, rows, :] = value
                if lon < 4:
                    new_low[pl.ds(lon * 64 + e * 32 + base, 8), :] = value
                else:
                    new_high[pl.ds((lon - 4) * 64 + e * 32 + base, 8), :] = value
        return carry

    lax.fori_loop(0, 4, levels, 0)
    packed[...] = pack(lambda q: field[2 * q : 2 * q + 2].reshape(128, 128), owner[...])


def on_device(
    control_static,
    control_ens,
    ens_perts,
    band_sqrt,
    band_owner,
    scale_class,
    static_scales,
    local_scales,
    obs_source,
    obs_column,
    obs_jac,
    innovation,
    obs_weight,
):
    tiles, levels = 64, 4
    upward = [(i, (i + 1) % tiles) for i in range(tiles)]
    downward = [(i, (i - 1) % tiles) for i in range(tiles)]

    def to_plane(value):
        return lax.all_to_all(value, PLANE, 0, 0, tiled=True)

    def to_all(value):
        return lax.all_to_all(value, ALL, 0, 0, tiled=True)

    here = jnp.stack([lax.axis_index("z"), lax.axis_index("yh") * 2 + lax.axis_index("core")]).astype(i32)
    scales = jnp.concatenate([static_scales, local_scales])
    owner = jnp.repeat(band_owner, 2).reshape(1, 128)

    packed, send_up, send_down, ens, perts = call(
        begin_kernel,
        [((512, 128), f32), ((776, 128), f32), ((776, 128), f32), ((8, 64, 128), f32), ((8, 128, 128), f32)],
        [((8, 64, 128), f32), ((1024, 128), f32)],
        total=5,
    )(
        owner,
        control_static.reshape(512, 128),
        control_ens.reshape(512, 128),
        ens_perts.reshape(128, 8, 128),
        scale_class,
    )

    jac = obs_jac.reshape(128, 64)
    shared = jnp.concatenate(
        [band_sqrt.reshape(64, 128), jnp.concatenate([jac[:64], jac[64:]], axis=1)], axis=0
    )
    blocks = [shared] + [
        lax.ppermute(shared, LEV, [(i, (i + k) % levels) for i in range(levels)]) for k in range(1, levels)
    ]
    whole = jnp.concatenate([block[:64] for block in blocks], axis=0)
    matrices = []
    for j in range(2):
        pairs = [
            (z * 4 + l, (2 * l + (j + z) % 2) * 4 + z // 2) for z in range(8) for l in range(4)
        ]
        matrices.append(lax.ppermute(whole, ("z",) + LEV, pairs))
    operators = [block[64:] for block in blocks]

    from_before = lax.ppermute(send_up, TILE, upward)
    from_after = lax.ppermute(send_down, TILE, downward)
    ens_before, perts_before, marks_before = from_before[:256], from_before[256:768], from_before[768:]
    ens_after, perts_after, marks_after = from_after[:256], from_after[256:768], from_after[768:]

    request, weights, targets = call(
        request_kernel,
        [((64, 128), i32), ((256, 256), f32), ((256, 256), f32)],
        smem=1,
        total=6,
    )(
        here,
        obs_source.reshape(1, 512),
        obs_source,
        obs_column.reshape(1, 512),
        obs_weight,
        innovation,
    )
    wanted = lax.all_to_all(request, TILE, 0, 0, tiled=True)

    state, out = call(
        first_columns_kernel,
        [((4, 128, 128), f32), ((512, 128), f32)],
        [((4, 128, 128), f32)],
        smem=1,
        total=4,
    )(here, to_plane(packed), *matrices)

    half_shape = ((4, 64, 128), f32)
    diffusion_scratch = [((2, 24, 128), f32), ((2, 5, 16, 128), f32), ((8, 64, 128), f32)]

    def halos(low, high):
        return lax.ppermute(high, TILE, upward), lax.ppermute(low, TILE, downward)

    for iteration in range(ITERS):
        low, high = call(edges_kernel, [half_shape, half_shape], total=2)(owner, to_plane(out))
        before, after = halos(low, high)
        (outgoing,) = call(observe_kernel, [((1024, 128), f32)], diffusion_scratch, smem=1, total=13)(
            scales, wanted, low, high, before, after, ens, ens_before, ens_after, perts,
            marks_before, scale_class, marks_after,
        )
        (returned,) = call(operators_kernel, [((1024, 128), f32)], [((4, 256, 128), f32)], smem=1, total=8)(
            here, to_all(outgoing), *operators, weights, targets
        )
        low, high = call(collect_kernel, [half_shape, half_shape], total=2)(wanted, to_all(returned))
        before, after = halos(low, high)
        packed, ens, ens_low, ens_high = call(
            pull_kernel,
            [((512, 128), f32), ((8, 64, 128), f32), ((256, 128), f32), ((256, 128), f32)],
            diffusion_scratch,
            smem=1,
            total=13,
        )(
            scales, owner, low, high, before, after, ens, perts, perts_before, perts_after,
            marks_before, scale_class, marks_after,
        )
        ens_before = lax.ppermute(ens_high, TILE, upward)
        ens_after = lax.ppermute(ens_low, TILE, downward)
        last = iteration == ITERS - 1
        results = call(
            functools.partial(columns_kernel, last),
            [((1024, 128), f32)] if last else [((4, 128, 128), f32), ((512, 128), f32)],
            [((4, 128, 128), f32)],
            smem=1,
            total=5,
        )(here, to_plane(packed), *matrices, state)
        if not last:
            state = results[0]
        out = results[-1]

    low, high, final_static = call(last_edges_kernel, [half_shape, half_shape, ((512, 128), f32)], total=2)(
        owner, to_plane(out)
    )
    before, after = halos(low, high)
    analysis, final_ens = call(
        last_kernel, [((512, 128), f32), ((512, 128), f32)], diffusion_scratch, smem=1, total=12
    )(
        scales, low, high, before, after, ens, ens_before, ens_after, perts, marks_before, scale_class, marks_after,
    )
    return tuple(value.reshape(2, 32, 8, 128) for value in (analysis, final_static, final_ens))


def solution(mesh):
    physical = Mesh(mesh.devices.reshape(8, 2, 4, 2, 2), ALL)
    return jax.shard_map(
        on_device,
        mesh=physical,
        in_specs=(
            P(None, LEV, TILE, None),
            P(None, LEV, TILE, None),
            P(None, None, LEV, TILE, None),
            P(TILE, None, LEV, None),
            P(),
            P(TILE, None),
            P(),
            P(),
            P(TILE, None),
            P(TILE),
            P(TILE, None, None, LEV),
            P(None, TILE),
            P(None, TILE),
        ),
        out_specs=(
            P(None, LEV, TILE, None),
            P(None, LEV, TILE, None),
            P(None, LEV, TILE, None),
        ),
        check_vma=False,
    )
```

```python
import functools

import jax
import jax.numpy as jnp
from jax import lax
from jax.experimental import pallas as pl
from jax.experimental.pallas import tpu as pltpu
from jax.sharding import Mesh, PartitionSpec as P

NSWEEP = 4
ITERS = 2

beta_static = 0.8
beta_ensemble = 0.6
step_length = 0.3

LEV = ("yh", "core")
TILE = ("z", "yl", "x")
PLANE = ("yl", "x", "yh", "core")
ALL = ("z", "yl", "x", "yh", "core")

f32, bf16, i32 = jnp.float32, jnp.bfloat16, jnp.int32


def iota(shape, dim):
    return lax.broadcasted_iota(i32, shape, dim)


def split(value):
    high = value.astype(bf16)
    return high, (value - high.astype(f32)).astype(bf16)


def dot_nn(a, b):
    return lax.dot_general(a, b, (((1,), (0,)), ((), ())), preferred_element_type=f32)


def dot_nt(a, b):
    return lax.dot_general(a, b, (((1,), (1,)), ((), ())), preferred_element_type=f32)


def dot_tn(a, b):
    return lax.dot_general(a, b, (((0,), (0,)), ((), ())), preferred_element_type=f32)


def three(dot, a, b):
    (ah, al), (bh, bl) = split(a), split(b)
    return dot(ah, bh) + (dot(ah, bl) + dot(al, bh))


def one_hot(mask):
    return jnp.where(mask, 1.0, 0.0).astype(bf16)


def call(kernel, outs, scratch=(), smem=0, total=0, flops=10**8, size=6 * 10**6):
    spaces = [pl.BlockSpec(memory_space=pltpu.SMEM)] * smem
    spaces += [pl.BlockSpec(memory_space=pltpu.VMEM)] * (total - smem)
    return pl.pallas_call(
        kernel,
        out_shape=[jax.ShapeDtypeStruct(shape, kind) for shape, kind in outs],
        in_specs=spaces,
        out_specs=[pl.BlockSpec(memory_space=pltpu.VMEM)] * len(outs),
        scratch_shapes=[pltpu.VMEM(shape, kind) for shape, kind in scratch],
        compiler_params=pltpu.CompilerParams(vmem_limit_bytes=24 * 2**20),
        cost_estimate=pl.CostEstimate(flops=flops, bytes_accessed=size, transcendentals=0),
    )


def selector(owner):
    row, lane = iota((512, 128), 0), iota((512, 128), 1)
    slot = (((row >> 4) & 3) * 2 + ((row >> 1) & 1)) * 8 + (row >> 6)
    hit = (owner == slot) & ((lane & 1) == (row & 1))
    pair = (row >> 2) & 3
    return jnp.concatenate([one_hot(hit & (pair == q)) for q in range(4)], axis=1)


def pack(field, owner):
    wide = jnp.concatenate([field(q) for q in range(4)], axis=1)
    high, low = split(wide)
    chosen = selector(owner)
    return dot_nt(chosen, high) + dot_nt(chosen, low)


def unpack(rows, owner):
    high, low = split(rows)
    chosen = selector(owner)
    return dot_tn(high, chosen) + dot_tn(low, chosen)


def begin_kernel(owner, static_in, ens_in, perts_in, classes, packed, up, down, ens, perts, work, flat):
    for lon in range(8):
        work[lon] = static_in[pl.ds(lon, 64, stride=8), :]
    packed[...] = pack(lambda q: work[2 * q : 2 * q + 2].reshape(128, 128), owner[...])
    flat[...] = perts_in[...].astype(f32).reshape(1024, 128)
    for lon in range(8):
        member = ens_in[pl.ds(lon, 64, stride=8), :]
        weight = flat[pl.ds(lon, 128, stride=8), :]
        ens[lon] = member
        perts[lon] = weight
        target, place = (down, lon) if lon < 4 else (up, lon - 4)
        target[place * 64 : place * 64 + 64] = member
        target[256 + place * 128 : 384 + place * 128] = weight
    marks = classes[...].astype(f32)
    up[768:776] = marks
    down[768:776] = marks


def request_kernel(source_row, column_row, request, ranks):
    source = source_row[...]
    mine = iota((64, 512), 0) == source
    marks = one_hot(mine)
    earlier = one_hot(iota((512, 512), 0) < iota((512, 512), 1))
    count = dot_nn(marks, earlier)
    rank = jnp.sum(jnp.where(mine, count, 0.0), axis=0, keepdims=True).astype(i32)
    ranks[...] = rank
    wanted = column_row[...] + 1
    ranked = one_hot(iota((128, 512), 0) == rank)
    high = jnp.where(mine, (wanted >> 5).astype(f32), 0.0).astype(bf16)
    low = jnp.where(mine, (wanted & 31).astype(f32), 0.0).astype(bf16)
    request[...] = (32.0 * dot_nt(high, ranked) + dot_nt(low, ranked)).astype(i32)


def slots_kernel(here, source_row, ranks, weight, innovation, weights, targets):
    level = here[1]
    source, rank = source_row[...], ranks[...]
    row = iota((256, 512), 0)
    weight_terms, innovation_terms = split(weight[...]), split(innovation[...])
    for half in range(2):
        place = level * 8 + (row >> 6) * 2 + half
        mine = one_hot(((row & 63) == source) & (rank == place))
        lanes = slice(half * 128, half * 128 + 128)
        weights[:, lanes] = dot_nt(mine, weight_terms[0]) + dot_nt(mine, weight_terms[1])
        targets[:, lanes] = dot_nt(mine, innovation_terms[0]) + dot_nt(mine, innovation_terms[1])


def load_matrices(here, first, second, matrices):
    z = here[0]
    for j, part in enumerate((first, second)):
        half = lax.rem(z + j, 2)
        for k in range(4):
            block = lax.bitwise_xor(lax.div(z, 2), k)
            rows = pl.ds(pl.multiple_of(block * 32, 32), 32)
            for var in range(2):
                start = k * 64 + var * 32
                matrices[half * 2 + var, rows, :] = part[start : start + 32]


def columns_of(rows):
    blocks = [
        jnp.concatenate([rows[u * 64 + l * 16 : u * 64 + l * 16 + 16] for u in range(8)], axis=0)
        for l in range(4)
    ]
    chunk = iota((128, 128), 1) >> 5
    out = []
    for c in range(4):
        joined = None
        for l in range(4):
            shift = (32 * (l - c)) % 128
            moved = pltpu.roll(blocks[l], shift, 1) if shift else blocks[l]
            joined = moved if l == 0 else jnp.where(chunk == l, moved, joined)
        out.append(joined)
    return out


def store_columns(out, columns, stride, offset):
    chunk = iota((128, 128), 1) >> 5
    for l in range(4):
        joined = None
        for c in range(4):
            shift = (32 * (c - l)) % 128
            moved = pltpu.roll(columns[c], shift, 1) if shift else columns[c]
            joined = moved if c == 0 else jnp.where(chunk == c, moved, joined)
        for u in range(8):
            start = (u * 4 + l) * stride + offset
            out[start : start + 16] = joined[u * 16 : u * 16 + 16]


def choose_half(product):
    half = (iota((256, 128), 0) >> 1) & 1
    return jnp.where(half == 0, product[:, :128], product[:, 128:])


def forward_columns(columns, matrices):
    out = [None] * 4
    for var in range(2):
        stacked = jnp.concatenate([columns[var], columns[2 + var]], axis=0)
        pair = jnp.concatenate([matrices[var], matrices[2 + var]], axis=0)
        chosen = choose_half(three(dot_nt, stacked, pair))
        out[var], out[2 + var] = chosen[:128], chosen[128:]
    return out


def backward_columns(columns, matrices):
    out = [None] * 4
    for var in range(2):
        stacked = jnp.concatenate([columns[var], columns[2 + var]], axis=0)
        pair = jnp.concatenate([matrices[var], matrices[2 + var]], axis=1)
        chosen = choose_half(three(dot_nn, stacked, pair))
        out[var], out[2 + var] = chosen[:128], chosen[128:]
    return out


def first_columns_kernel(here, rows, first, second, state, out, matrices):
    load_matrices(here, first, second, matrices)
    columns = columns_of(rows[...])
    for c in range(4):
        state[c] = columns[c]
    store_columns(out, forward_columns(columns, matrices), 16, 0)


def columns_kernel(last, here, rows, first, second, state, *refs):
    out, matrices = refs[-2], refs[-1]
    load_matrices(here, first, second, matrices)
    pulled = backward_columns(columns_of(rows[...]), matrices)
    columns = [(1.0 - step_length) * state[c] - step_length * pulled[c] for c in range(4)]
    forward = forward_columns(columns, matrices)
    if last:
        store_columns(out, forward, 32, 0)
        store_columns(out, columns, 32, 16)
    else:
        for c in range(4):
            refs[0][c] = columns[c]
        store_columns(out, forward, 16, 0)


def edges_kernel(owner, rows, low, high):
    wide = unpack(rows[...], owner[...])
    for lon in range(8):
        target, place = (low, lon) if lon < 4 else (high, lon - 4)
        q, side = lon // 2, lon % 2
        target[place] = wide[side * 64 : side * 64 + 64, q * 128 : q * 128 + 128]


def last_edges_kernel(owner, rows, low, high, final_static):
    both = rows[...]
    for kind in range(2):
        part = jnp.concatenate([both[p * 32 + kind * 16 : p * 32 + kind * 16 + 16] for p in range(32)], axis=0)
        wide = unpack(part, owner[...])
        for lon in range(8):
            q, side = lon // 2, lon % 2
            value = wide[side * 64 : side * 64 + 64, q * 128 : q * 128 + 128]
            if kind == 0:
                target, place = (low, lon) if lon < 4 else (high, lon - 4)
                target[place] = value
            else:
                final_static[pl.ds(lon, 64, stride=8), :] = value


def weights_kernel(scales, before, own, after, weights, kappa):
    marks = jnp.concatenate([before[...], own[...].astype(f32), after[...]], axis=0)
    lane = iota((16, 128), 1)
    for kind in range(2):
        value = jnp.zeros((24, 128), f32)
        for entry in range(8):
            value = jnp.where(marks == float(entry), scales[kind * 8 + entry], value)
        kappa[kind] = value
        centre = kappa[kind, 4:20]
        east = 0.5 * (centre + kappa[kind, 5:21])
        west = 0.5 * (kappa[kind, 3:19] + centre)
        north = jnp.where(lane < 127, 0.5 * (centre + pltpu.roll(centre, 127, 1)), 0.0)
        south = jnp.where(lane > 0, 0.5 * (centre + pltpu.roll(centre, 1, 1)), 0.0)
        weights[kind, 0] = east
        weights[kind, 1] = west
        weights[kind, 2] = north
        weights[kind, 3] = south
        weights[kind, 4] = 1.0 / (1.0 + east + west + north + south)


def neighbours(field, i, weight):
    return (
        weight(0, i) * field[i + 1]
        + weight(1, i) * field[i - 1]
        + weight(2, i) * pltpu.roll(field[i], 127, 1)
        + weight(3, i) * pltpu.roll(field[i], 1, 1)
    )


def diffuse(source, weight):
    current = dict(enumerate(source))
    for sweep in range(NSWEEP):
        current = {
            i: weight(4, i) * (source[i] + neighbours(current, i, weight))
            for i in range(sweep + 1, 15 - sweep)
        }
    return current


def diffuse_transposed(source, weight):
    carried = dict(enumerate(source))
    total = None
    for sweep in range(NSWEEP):
        scaled = {i: weight(4, i) * carried[i] for i in range(sweep, 16 - sweep)}
        total = {i: scaled[i] if total is None else total[i] + scaled[i] for i in range(4, 12)}
        carried = {i: neighbours(scaled, i, weight) for i in range(sweep + 1, 15 - sweep)}
    return {i: total[i] + carried[i] for i in range(4, 12)}


def weight_of(weights, kind):
    return lambda which, i: weights[kind, which, i : i + 1, :]


def wide_loader(before, low, high, after):
    parts = (before, low, high, after)
    return lambda rows: [parts[i // 4][i % 4, rows, :] for i in range(16)]


def members_kernel(ens, ens_before, ens_after, perts, weights, out):

    def ens_at(rows):
        return (
            [ens_before[pl.ds(i * 64 + rows, 8), :] for i in range(4)]
            + [ens[i, pl.ds(rows, 8), :] for i in range(8)]
            + [ens_after[pl.ds(i * 64 + rows, 8), :] for i in range(4)]
        )

    def levels(step, carry):
        base = pl.multiple_of(step * 8, 8)
        members = [diffuse(ens_at(e * 32 + base), weight_of(weights, 1)) for e in range(2)]
        for var in range(2):
            for lon in range(8):
                total = sum(
                    perts[lon, pl.ds((e * 2 + var) * 32 + base, 8), :] * members[e][lon + 4] for e in range(2)
                )
                out[lon, pl.ds(var * 32 + base, 8), :] = beta_ensemble * total
        return carry

    lax.fori_loop(0, 4, levels, 0)


def increments(loader, members, weights, target):

    def levels(step, carry):
        rows = pl.ds(pl.multiple_of(step * 8, 8), 8)
        smooth = diffuse(loader(rows), weight_of(weights, 0))
        for lon in range(8):
            target[lon, rows, :] = beta_static * smooth[lon + 4] + members[lon, rows, :]
        return carry

    lax.fori_loop(0, 8, levels, 0)


def hits_kernel(request, hits):
    wanted = request[...]
    high = (wanted >> 5).astype(f32).astype(bf16)
    low = (wanted & 31).astype(f32).astype(bf16)

    def block(step, carry):
        row = iota((256, 64), 0) + step * 256
        repeat = one_hot((row >> 4) == iota((256, 64), 1))
        spread = 32.0 * dot_nn(repeat, high) + dot_nn(repeat, low)
        lane, place = iota((256, 128), 1), (iota((256, 128), 0) & 15) * 2
        wide = iota((256, 256), 1)
        for half in range(2):
            column = (
                jnp.sum(jnp.where(lane == place + half, spread, 0.0), axis=1, keepdims=True).astype(i32) - 1
            )
            start = pl.multiple_of(half * 1024 + step * 256, 256)
            for q in range(4):
                hits[q, pl.ds(start, 256), :] = one_hot(column - q * 256 == wide)
        return carry

    lax.fori_loop(0, 4, block, 0)


def observe_kernel(low, high, before, after, members, weights, hits, out, field, terms):
    increments(wide_loader(before, low, high, after), members, weights, field)
    for q in range(4):
        pair = jnp.concatenate([field[2 * q], field[2 * q + 1]], axis=1)
        terms[q] = jnp.concatenate(split(pair), axis=0)

    def block(step, carry):
        sums = []
        for half in range(2):
            rows = pl.ds(pl.multiple_of(half * 1024 + step * 256, 256), 256)
            total = sum(dot_nt(hits[q, rows, :], terms[q]) for q in range(4))
            sums.append(total + pltpu.roll(total, 64, 1))
        out[pl.ds(pl.multiple_of(step * 256, 256), 256), :] = jnp.where(
            iota((256, 128), 1) < 64, sums[0], sums[1]
        )
        return carry

    lax.fori_loop(0, 4, block, 0)


def last_kernel(low, high, before, after, members, weights, ens, out, final_ens, field):
    increments(wide_loader(before, low, high, after), members, weights, field)
    for lon in range(8):
        out[pl.ds(lon, 64, stride=8), :] = field[lon]
        final_ens[pl.ds(lon, 64, stride=8), :] = ens[lon]


def operators_kernel(here, arrived, shared, weights, targets, out, operators):
    level = here[1]
    zero = jnp.zeros((64, 128), f32)
    for k in range(4):
        block = lax.bitwise_xor(level, k)
        value = shared[k * 128 + 64 : k * 128 + 128]
        operators[block, 0:64, 0:128] = value
        operators[block, 0:64, 128:256] = zero
        operators[block, 64:128, 0:128] = zero
        operators[block, 64:128, 128:256] = value
    observed = None
    for l in range(4):
        rows = jnp.concatenate([arrived[pl.ds(l * 4 + j, 64, stride=16), :] for j in range(4)], axis=0)
        part = three(dot_nn, rows, operators[l])
        observed = part if observed is None else observed + part
    departure = weights[...] * (observed - targets[...])
    for l in range(4):
        pulled = three(dot_nt, departure, operators[l])
        for j in range(4):
            out[pl.ds(l * 4 + j, 64, stride=16), :] = pulled[j * 64 : j * 64 + 64]


def collect_kernel(hits, arrived, low, high, turned):
    value = arrived[...]
    first = value.astype(bf16).astype(f32)
    rest = value - first
    lane = iota((1024, 128), 1) < 64
    stacked = jnp.concatenate(
        [
            jnp.where(lane, first, pltpu.roll(rest, 64, 1)),
            jnp.where(lane, pltpu.roll(first, 64, 1), rest),
        ],
        axis=0,
    )
    turned[...] = stacked.T.astype(bf16)
    for q in range(4):
        both = dot_nn(turned[...], hits[q])
        total = both[:64] + both[64:]
        target = low if q < 2 else high
        for side in range(2):
            target[(q % 2) * 2 + side] = total[:, side * 128 : side * 128 + 128]


def pull_kernel(owner, low, high, before, after, weights, packed, field):
    loader = wide_loader(before, low, high, after)

    def levels(step, carry):
        rows = pl.ds(pl.multiple_of(step * 8, 8), 8)
        smooth = diffuse_transposed([beta_static * value for value in loader(rows)], weight_of(weights, 0))
        for lon in range(8):
            field[lon, rows, :] = smooth[lon + 4]
        return carry

    lax.fori_loop(0, 8, levels, 0)
    packed[...] = pack(lambda q: field[2 * q : 2 * q + 2].reshape(128, 128), owner[...])


def pull_members_kernel(
    low, high, before, after, ens, perts, perts_before, perts_after, weights, new_ens, new_low, new_high
):
    loader = wide_loader(before, low, high, after)

    def perts_at(rows):
        return (
            [perts_before[pl.ds(i * 128 + rows, 8), :] for i in range(4)]
            + [perts[i, pl.ds(rows, 8), :] for i in range(8)]
            + [perts_after[pl.ds(i * 128 + rows, 8), :] for i in range(4)]
        )

    def levels(step, carry):
        base = pl.multiple_of(step * 8, 8)
        gradient = [loader(pl.ds(var * 32 + base, 8)) for var in range(2)]
        for e in range(2):
            factors = [perts_at((e * 2 + var) * 32 + base) for var in range(2)]
            mixed = [
                beta_ensemble * (factors[0][i] * gradient[0][i] + factors[1][i] * gradient[1][i]) for i in range(16)
            ]
            smooth = diffuse_transposed(mixed, weight_of(weights, 1))
            rows = pl.ds(e * 32 + base, 8)
            for lon in range(8):
                value = (1.0 - step_length) * ens[lon, rows, :] - step_length * smooth[lon + 4]
                new_ens[lon, rows, :] = value
                if lon < 4:
                    new_low[pl.ds(lon * 64 + e * 32 + base, 8), :] = value
                else:
                    new_high[pl.ds((lon - 4) * 64 + e * 32 + base, 8), :] = value
        return carry

    lax.fori_loop(0, 4, levels, 0)


def on_device(
    control_static,
    control_ens,
    ens_perts,
    band_sqrt,
    band_owner,
    scale_class,
    static_scales,
    local_scales,
    obs_source,
    obs_column,
    obs_jac,
    innovation,
    obs_weight,
):
    tiles = 64
    upward = [(i, (i + 1) % tiles) for i in range(tiles)]
    downward = [(i, (i - 1) % tiles) for i in range(tiles)]

    def to_plane(value):
        return lax.all_to_all(value, PLANE, 0, 0, tiled=True)

    def to_all(value):
        return lax.all_to_all(value, ALL, 0, 0, tiled=True)

    here = jnp.stack([lax.axis_index("z"), lax.axis_index("yh") * 2 + lax.axis_index("core")]).astype(i32)
    scales = jnp.concatenate([static_scales, local_scales])
    owner = jnp.repeat(band_owner, 2).reshape(1, 128)

    shared = jnp.concatenate(
        [band_sqrt.reshape(64, 128), jnp.transpose(obs_jac, (0, 2, 3, 1)).reshape(64, 128)], axis=0
    )
    swap = [(0, 1), (1, 0)]
    shared = jnp.concatenate([shared, lax.ppermute(shared, "core", swap)], axis=0)
    shared = jnp.concatenate([shared, lax.ppermute(shared, "yh", swap)], axis=0)
    whole = shared.reshape(4, 128, 128)[:, :64].reshape(256, 128)
    matrices = []
    for j in range(2):
        pairs = [
            (z * 4 + l, (2 * l + (j + z) % 2) * 4 + z // 2) for z in range(8) for l in range(4)
        ]
        matrices.append(lax.ppermute(whole, ("z",) + LEV, pairs))

    source_row = obs_source.reshape(1, 512)
    request, ranks = call(request_kernel, [((64, 128), i32), ((1, 512), i32)], total=2)(
        source_row, obs_column.reshape(1, 512)
    )
    wanted = lax.all_to_all(request, TILE, 0, 0, tiled=True)

    packed, send_up, send_down, ens, perts = call(
        begin_kernel,
        [((512, 128), f32), ((776, 128), f32), ((776, 128), f32), ((8, 64, 128), f32), ((8, 128, 128), f32)],
        [((8, 64, 128), f32), ((1024, 128), f32)],
        total=5,
    )(
        owner,
        control_static.reshape(512, 128),
        control_ens.reshape(512, 128),
        ens_perts.reshape(128, 8, 128),
        scale_class,
    )
    packed, wanted = lax.optimization_barrier((packed, wanted))
    from_before = lax.ppermute(send_up, TILE, upward)
    from_after = lax.ppermute(send_down, TILE, downward)
    ens_before, perts_before, marks_before = from_before[:256], from_before[256:768], from_before[768:]
    ens_after, perts_after, marks_after = from_after[:256], from_after[256:768], from_after[768:]

    state, out = call(
        first_columns_kernel,
        [((4, 128, 128), f32), ((512, 128), f32)],
        [((4, 128, 128), f32)],
        smem=1,
        total=4,
    )(here, to_plane(packed), *matrices)

    weights, targets = call(slots_kernel, [((256, 256), f32), ((256, 256), f32)], smem=1, total=5)(
        here, source_row, ranks, obs_weight, innovation
    )
    (faces,) = call(weights_kernel, [((2, 5, 16, 128), f32)], [((2, 24, 128), f32)], smem=1, total=4)(
        scales, marks_before, scale_class, marks_after
    )
    (hits,) = call(hits_kernel, [((4, 2048, 256), bf16)], total=1)(wanted)

    half_shape = ((4, 64, 128), f32)
    scratch = ((8, 64, 128), f32)

    def halos(low, high):
        return lax.ppermute(high, TILE, upward), lax.ppermute(low, TILE, downward)

    def members_of(ens, ens_before, ens_after):
        return call(members_kernel, [((8, 64, 128), f32)], total=5)(ens, ens_before, ens_after, perts, faces)[0]

    for iteration in range(ITERS):
        low, high = call(edges_kernel, [half_shape, half_shape], total=2)(owner, to_plane(out))
        before, after = halos(low, high)
        members = members_of(ens, ens_before, ens_after)
        (outgoing,) = call(
            observe_kernel, [((1024, 128), f32)], [scratch, ((4, 128, 256), bf16)], total=7
        )(low, high, before, after, members, faces, hits)
        (returned,) = call(operators_kernel, [((1024, 128), f32)], [((4, 128, 256), f32)], smem=1, total=5)(
            here, to_all(outgoing), shared, weights, targets
        )
        low, high = call(collect_kernel, [half_shape, half_shape], [((128, 2048), bf16)], total=2)(
            hits, to_all(returned)
        )
        before, after = halos(low, high)
        (packed,) = call(pull_kernel, [((512, 128), f32)], [scratch], total=6)(owner, low, high, before, after, faces)
        ens, ens_low, ens_high = call(
            pull_members_kernel, [((8, 64, 128), f32), ((256, 128), f32), ((256, 128), f32)], total=9
        )(low, high, before, after, ens, perts, perts_before, perts_after, faces)
        ens_before = lax.ppermute(ens_high, TILE, upward)
        ens_after = lax.ppermute(ens_low, TILE, downward)
        last = iteration == ITERS - 1
        results = call(
            functools.partial(columns_kernel, last),
            [((1024, 128), f32)] if last else [((4, 128, 128), f32), ((512, 128), f32)],
            [((4, 128, 128), f32)],
            smem=1,
            total=5,
        )(here, to_plane(packed), *matrices, state)
        if not last:
            state = results[0]
        out = results[-1]

    low, high, final_static = call(last_edges_kernel, [half_shape, half_shape, ((512, 128), f32)], total=2)(
        owner, to_plane(out)
    )
    before, after = halos(low, high)
    members = members_of(ens, ens_before, ens_after)
    analysis, final_ens = call(last_kernel, [((512, 128), f32), ((512, 128), f32)], [scratch], total=7)(
        low, high, before, after, members, faces, ens
    )
    return tuple(value.reshape(2, 32, 8, 128) for value in (analysis, final_static, final_ens))


def solution(mesh):
    physical = Mesh(mesh.devices.reshape(8, 2, 4, 2, 2), ALL)
    return jax.shard_map(
        on_device,
        mesh=physical,
        in_specs=(
            P(None, LEV, TILE, None),
            P(None, LEV, TILE, None),
            P(None, None, LEV, TILE, None),
            P(TILE, None, LEV, None),
            P(),
            P(TILE, None),
            P(),
            P(),
            P(TILE, None),
            P(TILE),
            P(TILE, None, None, LEV),
            P(None, TILE),
            P(None, TILE),
        ),
        out_specs=(
            P(None, LEV, TILE, None),
            P(None, LEV, TILE, None),
            P(None, LEV, TILE, None),
        ),
        check_vma=False,
    )
```

```python
import functools

import jax
import jax.numpy as jnp
from jax import lax
from jax.experimental import pallas as pl
from jax.experimental.pallas import tpu as pltpu
from jax.sharding import Mesh, PartitionSpec as P

NSWEEP = 4
ITERS = 2

beta_static = 0.8
beta_ensemble = 0.6
step_length = 0.3

LEV = ("yh", "core")
TILE = ("z", "yl", "x")
PLANE = ("yl", "x", "yh", "core")
AXES = ("z", "yl", "x", "yh", "core")

f32, bf16, i32 = jnp.float32, jnp.bfloat16, jnp.int32


def iota(shape, dim):
    return lax.broadcasted_iota(i32, shape, dim)


def split(value):
    high = value.astype(bf16)
    return high, (value - high.astype(f32)).astype(bf16)


def dot_nn(a, b):
    return lax.dot_general(a, b, (((1,), (0,)), ((), ())), preferred_element_type=f32)


def dot_nt(a, b):
    return lax.dot_general(a, b, (((1,), (1,)), ((), ())), preferred_element_type=f32)


def dot_tn(a, b):
    return lax.dot_general(a, b, (((0,), (0,)), ((), ())), preferred_element_type=f32)


def three(dot, a, b):
    (ah, al), (bh, bl) = split(a), split(b)
    return dot(ah, bh) + (dot(ah, bl) + dot(al, bh))


def one_hot(mask):
    return jnp.where(mask, 1.0, 0.0).astype(bf16)


def call(kernel, outs, scratch=(), smem=0, total=0, flops=10**8, size=6 * 10**6):
    spaces = [pl.BlockSpec(memory_space=pltpu.SMEM)] * smem
    spaces += [pl.BlockSpec(memory_space=pltpu.VMEM)] * (total - smem)
    return pl.pallas_call(
        kernel,
        out_shape=[jax.ShapeDtypeStruct(shape, kind) for shape, kind in outs],
        in_specs=spaces,
        out_specs=[pl.BlockSpec(memory_space=pltpu.VMEM)] * len(outs),
        scratch_shapes=[pltpu.VMEM(shape, kind) for shape, kind in scratch],
        compiler_params=pltpu.CompilerParams(vmem_limit_bytes=24 * 2**20),
        cost_estimate=pl.CostEstimate(flops=flops, bytes_accessed=size, transcendentals=0),
    )


def selector(owner):
    row, lane = iota((512, 128), 0), iota((512, 128), 1)
    slot = (((row >> 4) & 3) * 2 + ((row >> 1) & 1)) * 8 + (row >> 6)
    hit = (owner == slot) & ((lane & 1) == (row & 1))
    pair = (row >> 2) & 3
    return jnp.concatenate([one_hot(hit & (pair == q)) for q in range(4)], axis=1)


def pack(field, owner):
    wide = jnp.concatenate([field(q) for q in range(4)], axis=1)
    high, low = split(wide)
    chosen = selector(owner)
    return dot_nt(chosen, high) + dot_nt(chosen, low)


def unpack(rows, owner):
    high, low = split(rows)
    chosen = selector(owner)
    return dot_tn(high, chosen) + dot_tn(low, chosen)


def begin_kernel(owner, static_in, packed, work):
    for lon in range(8):
        work[lon] = static_in[pl.ds(lon, 64, stride=8), :]
    packed[...] = pack(lambda q: work[2 * q : 2 * q + 2].reshape(128, 128), owner[...])


def begin_members_kernel(ens_in, perts_in, classes, up, down, ens, perts, flat):
    flat[...] = perts_in[...].astype(f32).reshape(1024, 128)
    for lon in range(8):
        member = ens_in[pl.ds(lon, 64, stride=8), :]
        ens[lon] = member
        perts[lon] = flat[pl.ds(lon, 128, stride=8), :]
        target, place = (down, lon) if lon < 4 else (up, lon - 4)
        target[place * 64 : place * 64 + 64] = member
    marks = classes[...].astype(f32)
    up[256:264] = marks
    down[256:264] = marks


def request_kernel(source_row, column_row, request, ranks):
    source = source_row[...]
    mine = iota((64, 512), 0) == source
    marks = one_hot(mine)
    earlier = one_hot(iota((512, 512), 0) < iota((512, 512), 1))
    count = dot_nn(marks, earlier)
    rank = jnp.sum(jnp.where(mine, count, 0.0), axis=0, keepdims=True).astype(i32)
    ranks[...] = rank
    wanted = column_row[...] + 1
    ranked = one_hot(iota((128, 512), 0) == rank)
    high = jnp.where(mine, (wanted >> 5).astype(f32), 0.0).astype(bf16)
    low = jnp.where(mine, (wanted & 31).astype(f32), 0.0).astype(bf16)
    request[...] = 32.0 * dot_nt(high, ranked) + dot_nt(low, ranked)


def slots_kernel(here, source_row, ranks, weight, innovation, first, second):
    z, level = here[0], here[1]
    source, rank = source_row[...], ranks[...]
    row = iota((512, 512), 0)
    place = (row >> 3) == source
    kind = (row >> 2) & 1
    terms = split(jnp.concatenate([weight[...], innovation[...]], axis=1))
    for j, target in enumerate((first, second)):
        group = 2 * level + lax.rem(z + j, 2)
        mine = place & (rank == group * 4 + (row & 3))
        hits = jnp.concatenate([one_hot(mine & (kind == w)) for w in range(2)], axis=1)
        target[...] = dot_nt(hits, terms[0]) + dot_nt(hits, terms[1])


def arrange_kernel(arrived, wanted, weights, targets):
    wanted[...] = arrived[pl.ds(16, 64, stride=24), :].astype(i32)
    for half in range(2):
        for u in range(8):
            for z in range(8):
                start = (z * 8 + u) * 24 + ((half + z) % 2) * 8
                weights[half * 8 + u, 4 * z : 4 * z + 4] = arrived[start : start + 4]
                targets[half * 8 + u, 4 * z : 4 * z + 4] = arrived[start + 4 : start + 8]


def load_matrices(here, first, second, matrices):
    z = here[0]
    for j, part in enumerate((first, second)):
        half = lax.rem(z + j, 2)
        for k in range(4):
            block = lax.bitwise_xor(lax.div(z, 2), k)
            rows = pl.ds(pl.multiple_of(block * 32, 32), 32)
            for var in range(2):
                start = k * 128 + var * 32
                matrices[half * 2 + var, rows, :] = part[start : start + 32]


def columns_of(rows):
    blocks = [
        jnp.concatenate([rows[u * 64 + l * 16 : u * 64 + l * 16 + 16] for u in range(8)], axis=0)
        for l in range(4)
    ]
    chunk = iota((128, 128), 1) >> 5
    out = []
    for c in range(4):
        joined = None
        for l in range(4):
            shift = (32 * (l - c)) % 128
            moved = pltpu.roll(blocks[l], shift, 1) if shift else blocks[l]
            joined = moved if l == 0 else jnp.where(chunk == l, moved, joined)
        out.append(joined)
    return out


def store_columns(out, columns, stride, offset):
    chunk = iota((128, 128), 1) >> 5
    for l in range(4):
        joined = None
        for c in range(4):
            shift = (32 * (c - l)) % 128
            moved = pltpu.roll(columns[c], shift, 1) if shift else columns[c]
            joined = moved if c == 0 else jnp.where(chunk == c, moved, joined)
        for u in range(8):
            start = (u * 4 + l) * stride + offset
            out[start : start + 16] = joined[u * 16 : u * 16 + 16]


def choose_half(product):
    half = (iota((256, 128), 0) >> 1) & 1
    return jnp.where(half == 0, product[:, :128], product[:, 128:])


def forward_columns(columns, matrices):
    out = [None] * 4
    for var in range(2):
        stacked = jnp.concatenate([columns[var], columns[2 + var]], axis=0)
        pair = jnp.concatenate([matrices[var], matrices[2 + var]], axis=0)
        chosen = choose_half(three(dot_nt, stacked, pair))
        out[var], out[2 + var] = chosen[:128], chosen[128:]
    return out


def backward_columns(columns, matrices):
    out = [None] * 4
    for var in range(2):
        stacked = jnp.concatenate([columns[var], columns[2 + var]], axis=0)
        pair = jnp.concatenate([matrices[var], matrices[2 + var]], axis=1)
        chosen = choose_half(three(dot_nn, stacked, pair))
        out[var], out[2 + var] = chosen[:128], chosen[128:]
    return out


def first_columns_kernel(here, rows, first, second, state, out, matrices):
    load_matrices(here, first, second, matrices)
    columns = columns_of(rows[...])
    for c in range(4):
        state[c] = columns[c]
    store_columns(out, forward_columns(columns, matrices), 16, 0)


def columns_kernel(last, here, rows, first, second, state, *refs):
    out, matrices = refs[-2], refs[-1]
    load_matrices(here, first, second, matrices)
    pulled = backward_columns(columns_of(rows[...]), matrices)
    columns = [(1.0 - step_length) * state[c] - step_length * pulled[c] for c in range(4)]
    forward = forward_columns(columns, matrices)
    if last:
        store_columns(out, forward, 32, 0)
        store_columns(out, columns, 32, 16)
    else:
        for c in range(4):
            refs[0][c] = columns[c]
        store_columns(out, forward, 16, 0)


def edges_kernel(owner, rows, low, high):
    wide = unpack(rows[...], owner[...])
    for lon in range(8):
        target, place = (low, lon) if lon < 4 else (high, lon - 4)
        q, side = lon // 2, lon % 2
        target[place] = wide[side * 64 : side * 64 + 64, q * 128 : q * 128 + 128]


def last_edges_kernel(owner, rows, low, high, final_static):
    both = rows[...]
    for kind in range(2):
        part = jnp.concatenate([both[p * 32 + kind * 16 : p * 32 + kind * 16 + 16] for p in range(32)], axis=0)
        wide = unpack(part, owner[...])
        for lon in range(8):
            q, side = lon // 2, lon % 2
            value = wide[side * 64 : side * 64 + 64, q * 128 : q * 128 + 128]
            if kind == 0:
                target, place = (low, lon) if lon < 4 else (high, lon - 4)
                target[place] = value
            else:
                final_static[pl.ds(lon, 64, stride=8), :] = value


def weights_kernel(scales, before, own, after, weights, kappa):
    marks = jnp.concatenate([before[...], own[...].astype(f32), after[...]], axis=0)
    lane = iota((16, 128), 1)
    for kind in range(2):
        value = jnp.zeros((24, 128), f32)
        for entry in range(8):
            value = jnp.where(marks == float(entry), scales[kind * 8 + entry], value)
        kappa[kind] = value
        centre = kappa[kind, 4:20]
        east = 0.5 * (centre + kappa[kind, 5:21])
        west = 0.5 * (kappa[kind, 3:19] + centre)
        north = jnp.where(lane < 127, 0.5 * (centre + pltpu.roll(centre, 127, 1)), 0.0)
        south = jnp.where(lane > 0, 0.5 * (centre + pltpu.roll(centre, 1, 1)), 0.0)
        weights[kind, 0] = east
        weights[kind, 1] = west
        weights[kind, 2] = north
        weights[kind, 3] = south
        weights[kind, 4] = 1.0 / (1.0 + east + west + north + south)


def neighbours(field, i, weight):
    return (
        weight(0, i) * field[i + 1]
        + weight(1, i) * field[i - 1]
        + weight(2, i) * pltpu.roll(field[i], 127, 1)
        + weight(3, i) * pltpu.roll(field[i], 1, 1)
    )


def diffuse(source, weight):
    current = dict(enumerate(source))
    for sweep in range(NSWEEP):
        current = {
            i: weight(4, i) * (source[i] + neighbours(current, i, weight))
            for i in range(sweep + 1, 15 - sweep)
        }
    return current


def diffuse_transposed(source, weight):
    carried = dict(enumerate(source))
    total = None
    for sweep in range(NSWEEP):
        scaled = {i: weight(4, i) * carried[i] for i in range(sweep, 16 - sweep)}
        total = {i: scaled[i] if total is None else total[i] + scaled[i] for i in range(4, 12)}
        carried = {i: neighbours(scaled, i, weight) for i in range(sweep + 1, 15 - sweep)}
    return {i: total[i] + carried[i] for i in range(4, 12)}


def weight_of(weights, kind):
    return lambda which, i: weights[kind, which, i : i + 1, :]


def wide_loader(before, low, high, after):
    parts = (before, low, high, after)
    return lambda rows: [parts[i // 4][i % 4, rows, :] for i in range(16)]


def members_kernel(ens, ens_before, ens_after, perts, weights, out):

    def ens_at(rows):
        return (
            [ens_before[pl.ds(i * 64 + rows, 8), :] for i in range(4)]
            + [ens[i, pl.ds(rows, 8), :] for i in range(8)]
            + [ens_after[pl.ds(i * 64 + rows, 8), :] for i in range(4)]
        )

    def levels(step, carry):
        base = pl.multiple_of(step * 8, 8)
        members = [diffuse(ens_at(e * 32 + base), weight_of(weights, 1)) for e in range(2)]
        for var in range(2):
            for lon in range(8):
                total = sum(
                    perts[lon, pl.ds((e * 2 + var) * 32 + base, 8), :] * members[e][lon + 4] for e in range(2)
                )
                out[lon, pl.ds(var * 32 + base, 8), :] = beta_ensemble * total
        return carry

    lax.fori_loop(0, 4, levels, 0)


def increments(loader, members, weights, target):

    def levels(step, carry):
        for var in range(2):
            rows = pl.ds(pl.multiple_of(var * 32 + step * 8, 8), 8)
            smooth = diffuse(loader(rows), weight_of(weights, 0))
            for lon in range(8):
                target[lon, rows, :] = beta_static * smooth[lon + 4] + members[lon, rows, :]
        return carry

    lax.fori_loop(0, 4, levels, 0)


def slot_columns(high, low, start, count, half):
    row = iota((count, 64), 0) + start
    repeat = one_hot((row >> 4) == iota((count, 64), 1))
    spread = 32.0 * dot_nn(repeat, high) + dot_nn(repeat, low)
    place = (iota((count, 128), 0) & 15) + half * 16
    return jnp.sum(jnp.where(iota((count, 128), 1) == place, spread, 0.0), axis=1, keepdims=True).astype(i32) - 1


def observe_kernel(request, low, high, before, after, members, weights, out, field, terms):
    increments(wide_loader(before, low, high, after), members, weights, field)
    for q in range(4):
        pair = jnp.concatenate([field[2 * q], field[2 * q + 1]], axis=1)
        terms[q] = jnp.concatenate(split(pair), axis=0)
    wanted = request[...]
    first, second = (wanted >> 5).astype(f32).astype(bf16), (wanted & 31).astype(f32).astype(bf16)
    wide = iota((512, 256), 1)

    def block(step, carry):
        start = pl.multiple_of(step * 512, 512)
        sums = []
        for half in range(2):
            column = slot_columns(first, second, start, 512, half)
            total = sum(dot_nt(one_hot(column - q * 256 == wide), terms[q]) for q in range(4))
            sums.append(total + pltpu.roll(total, 64, 1))
        out[pl.ds(start, 512), :] = jnp.where(iota((512, 128), 1) < 64, sums[0], sums[1])
        return carry

    lax.fori_loop(0, 2, block, 0)


def last_kernel(low, high, before, after, members, weights, ens, out, final_ens, field):
    increments(wide_loader(before, low, high, after), members, weights, field)
    for lon in range(8):
        out[pl.ds(lon, 64, stride=8), :] = field[lon]
        final_ens[pl.ds(lon, 64, stride=8), :] = ens[lon]


def operators_kernel(here, arrived, jacobians, weights, targets, out, columns, pulled):
    z = here[0]
    lane = iota((256, 128), 1) < 64
    for pair in range(2):
        even, odd = arrived[pair * 512 : pair * 512 + 256], arrived[pair * 512 + 256 : pair * 512 + 512]
        lanes = slice(pair * 128, pair * 128 + 128)
        columns[0, :, lanes] = jnp.where(lane, even, pltpu.roll(odd, 64, 1))
        columns[1, :, lanes] = jnp.where(lane, pltpu.roll(even, 64, 1), odd)

    def tile(u, carry):
        for half in range(2):
            j = lax.rem(z + half, 2)
            rows = pl.ds(pl.multiple_of((half * 8 + u) * 16, 16), 16)
            operator = jnp.concatenate(
                [jacobians[u, j, lax.bitwise_xor(lax.div(z, 2), l)] for l in range(4)], axis=0
            )
            values = jnp.concatenate([columns[0, rows, :], columns[1, rows, :]], axis=0)
            observed = three(dot_nn, values, operator)
            departure = weights[half * 8 + u] * (observed - targets[half * 8 + u])
            back = three(dot_nt, departure, operator)
            pulled[0, rows, :] = back[:16]
            pulled[1, rows, :] = back[16:]
        return carry

    lax.fori_loop(0, 8, tile, 0)
    for pair in range(2):
        lanes = slice(pair * 128, pair * 128 + 128)
        first, second = pulled[0, :, lanes], pulled[1, :, lanes]
        out[pair * 512 : pair * 512 + 256] = jnp.where(lane, first, pltpu.roll(second, 64, 1))
        out[pair * 512 + 256 : pair * 512 + 512] = jnp.where(lane, pltpu.roll(first, 64, 1), second)


def collect_kernel(request, arrived, perts, low, high, turned):
    value = arrived[...]
    first = value.astype(bf16).astype(f32)
    rest = value - first
    lane = iota((1024, 128), 1) < 64
    stacked = jnp.concatenate(
        [
            jnp.where(lane, first, pltpu.roll(rest, 64, 1)),
            jnp.where(lane, pltpu.roll(first, 64, 1), rest),
        ],
        axis=0,
    )
    turned[...] = stacked.T.astype(bf16)
    wanted = request[...]
    upper, lower = (wanted >> 5).astype(f32).astype(bf16), (wanted & 31).astype(f32).astype(bf16)
    columns = [slot_columns(upper, lower, 0, 1024, half) for half in range(2)]
    wide = iota((1024, 256), 1)
    for q in range(4):
        hits = jnp.concatenate([one_hot(columns[half] - q * 256 == wide) for half in range(2)], axis=0)
        both = dot_nn(turned[...], hits)
        total = both[:64] + both[64:]
        target = low if q < 2 else high
        for side in range(2):
            place = (q % 2) * 2 + side
            gradient = total[:, side * 128 : side * 128 + 128]
            target[place, 0:64] = gradient
            factor = perts[2 * q + side]
            for e in range(2):
                mixed = factor[e * 64 : e * 64 + 32] * gradient[:32] + factor[e * 64 + 32 : e * 64 + 64] * gradient[32:]
                target[place, 64 + e * 32 : 96 + e * 32] = beta_ensemble * mixed


def pull_kernel(owner, low, high, before, after, weights, packed, field):
    loader = wide_loader(before, low, high, after)

    def levels(step, carry):
        for var in range(2):
            rows = pl.ds(pl.multiple_of(var * 32 + step * 8, 8), 8)
            smooth = diffuse_transposed([beta_static * value for value in loader(rows)], weight_of(weights, 0))
            for lon in range(8):
                field[lon, rows, :] = smooth[lon + 4]
        return carry

    lax.fori_loop(0, 4, levels, 0)
    packed[...] = pack(lambda q: field[2 * q : 2 * q + 2].reshape(128, 128), owner[...])


def pull_members_kernel(low, high, before, after, ens, weights, new_ens, new_low, new_high):
    loader = wide_loader(before, low, high, after)

    def levels(step, carry):
        for e in range(2):
            base = pl.multiple_of(e * 32 + step * 8, 8)
            smooth = diffuse_transposed(loader(pl.ds(64 + base, 8)), weight_of(weights, 1))
            for lon in range(8):
                value = (1.0 - step_length) * ens[lon, pl.ds(base, 8), :] - step_length * smooth[lon + 4]
                new_ens[lon, pl.ds(base, 8), :] = value
                if lon < 4:
                    new_low[pl.ds(lon * 64 + base, 8), :] = value
                else:
                    new_high[pl.ds((lon - 4) * 64 + base, 8), :] = value
        return carry

    lax.fori_loop(0, 4, levels, 0)


def on_device(
    control_static,
    control_ens,
    ens_perts,
    band_sqrt,
    band_owner,
    scale_class,
    static_scales,
    local_scales,
    obs_source,
    obs_column,
    obs_jac,
    innovation,
    obs_weight,
):
    tiles = 64
    upward = [(i, (i + 1) % tiles) for i in range(tiles)]
    downward = [(i, (i - 1) % tiles) for i in range(tiles)]

    def to_plane(value):
        return lax.all_to_all(value, PLANE, 0, 0, tiled=True)

    def to_levels(value):
        return lax.all_to_all(value, LEV, 0, 0, tiled=True)

    here = jnp.stack([lax.axis_index("z"), lax.axis_index("yh") * 2 + lax.axis_index("core")]).astype(i32)
    scales = jnp.concatenate([static_scales, local_scales])
    owner = jnp.repeat(band_owner, 2).reshape(1, 128)

    shared = jnp.concatenate(
        [band_sqrt.reshape(64, 128), jnp.transpose(obs_jac, (0, 2, 3, 1)).reshape(64, 128)], axis=0
    )
    swap = [(0, 1), (1, 0)]
    shared = jnp.concatenate([shared, lax.ppermute(shared, "core", swap)], axis=0)
    shared = jnp.concatenate([shared, lax.ppermute(shared, "yh", swap)], axis=0)
    exchange = [(z * 4 + l, (2 * l + (j + z) % 2) * 4 + z // 2) for j in range(2) for z in range(8) for l in range(4)]

    def spread(value, j):
        return lax.ppermute(value, ("z",) + LEV, exchange[j * 32 : j * 32 + 32])

    matrices = [spread(shared, j) for j in range(2)]
    jacobians = jnp.stack([part.reshape(4, 128, 128)[:, 64:] for part in matrices]).reshape(512, 128)
    jacobians = lax.all_gather(jacobians, ("yl", "x"), axis=0, tiled=True).reshape(8, 2, 4, 64, 128)

    (packed,) = call(begin_kernel, [((512, 128), f32)], [((8, 64, 128), f32)], total=2)(
        owner, control_static.reshape(512, 128)
    )
    arrived = to_plane(packed)
    source_row, arrived, control_ens = lax.optimization_barrier((obs_source.reshape(1, 512), arrived, control_ens))

    send_up, send_down, ens, perts = call(
        begin_members_kernel,
        [((264, 128), f32), ((264, 128), f32), ((8, 64, 128), f32), ((8, 128, 128), f32)],
        [((1024, 128), f32)],
        total=3,
    )(control_ens.reshape(512, 128), ens_perts.reshape(128, 8, 128), scale_class)
    from_before = lax.ppermute(send_up, TILE, upward)
    from_after = lax.ppermute(send_down, TILE, downward)
    ens_before, marks_before = from_before[:256], from_before[256:]
    ens_after, marks_after = from_after[:256], from_after[256:]

    request, ranks = call(request_kernel, [((64, 128), f32), ((1, 512), i32)], total=2)(
        source_row, obs_column.reshape(1, 512)
    )
    slots = call(slots_kernel, [((512, 128), f32), ((512, 128), f32)], smem=1, total=5)(
        here, source_row, ranks, obs_weight, innovation
    )
    sent = jnp.concatenate(
        [spread(slots[j], j).reshape(64, 8, 128) for j in range(2)]
        + [jnp.pad(request.reshape(64, 1, 128), ((0, 0), (0, 7), (0, 0)))],
        axis=1,
    ).reshape(1536, 128)
    orders = lax.all_to_all(sent, TILE, 0, 0, tiled=True)
    arrived, orders = lax.optimization_barrier((arrived, orders))
    wanted, weights, targets = call(
        arrange_kernel, [((64, 128), i32), ((16, 32, 128), f32), ((16, 32, 128), f32)], total=1
    )(orders)

    state, out = call(
        first_columns_kernel,
        [((4, 128, 128), f32), ((512, 128), f32)],
        [((4, 128, 128), f32)],
        smem=1,
        total=4,
    )(here, arrived, *matrices)

    (faces,) = call(weights_kernel, [((2, 5, 16, 128), f32)], [((2, 24, 128), f32)], smem=1, total=4)(
        scales, marks_before, scale_class, marks_after
    )

    half_shape = ((4, 64, 128), f32)
    mixed_shape = ((4, 128, 128), f32)
    scratch = ((8, 64, 128), f32)

    def halos(low, high):
        return lax.ppermute(high, TILE, upward), lax.ppermute(low, TILE, downward)

    def members_of(ens, ens_before, ens_after):
        return call(members_kernel, [((8, 64, 128), f32)], total=5)(ens, ens_before, ens_after, perts, faces)[0]

    for iteration in range(ITERS):
        low, high = call(edges_kernel, [half_shape, half_shape], total=2)(owner, to_plane(out))
        before, after = halos(low, high)
        members = members_of(ens, ens_before, ens_after)
        (outgoing,) = call(
            observe_kernel, [((1024, 128), f32)], [scratch, ((4, 128, 256), bf16)], total=7
        )(wanted, low, high, before, after, members, faces)
        (returned,) = call(
            operators_kernel,
            [((1024, 128), f32)],
            [((2, 256, 256), f32), ((2, 256, 256), f32)],
            smem=1,
            total=5,
        )(here, to_levels(outgoing), jacobians, weights, targets)
        low, high = call(collect_kernel, [mixed_shape, mixed_shape], [((128, 2048), bf16)], total=3)(
            wanted, to_levels(returned), perts
        )
        before, after = halos(low, high)
        (packed,) = call(pull_kernel, [((512, 128), f32)], [scratch], total=6)(owner, low, high, before, after, faces)
        ens, ens_low, ens_high = call(
            pull_members_kernel, [((8, 64, 128), f32), ((256, 128), f32), ((256, 128), f32)], total=6
        )(low, high, before, after, ens, faces)
        ens_before = lax.ppermute(ens_high, TILE, upward)
        ens_after = lax.ppermute(ens_low, TILE, downward)
        last = iteration == ITERS - 1
        results = call(
            functools.partial(columns_kernel, last),
            [((1024, 128), f32)] if last else [((4, 128, 128), f32), ((512, 128), f32)],
            [((4, 128, 128), f32)],
            smem=1,
            total=5,
        )(here, to_plane(packed), *matrices, state)
        if not last:
            state = results[0]
        out = results[-1]

    low, high, final_static = call(last_edges_kernel, [half_shape, half_shape, ((512, 128), f32)], total=2)(
        owner, to_plane(out)
    )
    before, after = halos(low, high)
    members = members_of(ens, ens_before, ens_after)
    analysis, final_ens = call(last_kernel, [((512, 128), f32), ((512, 128), f32)], [scratch], total=7)(
        low, high, before, after, members, faces, ens
    )
    return tuple(value.reshape(2, 32, 8, 128) for value in (analysis, final_static, final_ens))


def solution(mesh):
    physical = Mesh(mesh.devices.reshape(8, 2, 4, 2, 2), AXES)
    return jax.shard_map(
        on_device,
        mesh=physical,
        in_specs=(
            P(None, LEV, TILE, None),
            P(None, LEV, TILE, None),
            P(None, None, LEV, TILE, None),
            P(TILE, None, LEV, None),
            P(),
            P(TILE, None),
            P(),
            P(),
            P(TILE, None),
            P(TILE),
            P(TILE, None, None, LEV),
            P(None, TILE),
            P(None, TILE),
        ),
        out_specs=(
            P(None, LEV, TILE, None),
            P(None, LEV, TILE, None),
            P(None, LEV, TILE, None),
        ),
        check_vma=False,
    )
```

```python
import functools

import jax
import jax.numpy as jnp
from jax import lax
from jax.experimental import pallas as pl
from jax.experimental.pallas import tpu as pltpu
from jax.sharding import Mesh, PartitionSpec as P

NSWEEP = 4
ITERS = 2

beta_static = 0.8
beta_ensemble = 0.6
step_length = 0.3

LEV = ("yh", "core")
TILE = ("z", "yl", "x")
PLANE = ("yl", "x", "yh", "core")
AXES = ("z", "yl", "x", "yh", "core")

f32, bf16, i32 = jnp.float32, jnp.bfloat16, jnp.int32


def iota(shape, dim):
    return lax.broadcasted_iota(i32, shape, dim)


def split(value):
    high = value.astype(bf16)
    return high, (value - high.astype(f32)).astype(bf16)


def dot_nn(a, b):
    return lax.dot_general(a, b, (((1,), (0,)), ((), ())), preferred_element_type=f32)


def dot_nt(a, b):
    return lax.dot_general(a, b, (((1,), (1,)), ((), ())), preferred_element_type=f32)


def dot_tn(a, b):
    return lax.dot_general(a, b, (((0,), (0,)), ((), ())), preferred_element_type=f32)


def three(dot, a, b):
    (ah, al), (bh, bl) = split(a), split(b)
    return dot(ah, bh) + (dot(ah, bl) + dot(al, bh))


def one_hot(mask):
    return jnp.where(mask, 1.0, 0.0).astype(bf16)


def call(kernel, outs, scratch=(), smem=0, total=0, flops=10**8, size=6 * 10**6):
    spaces = [pl.BlockSpec(memory_space=pltpu.SMEM)] * smem
    spaces += [pl.BlockSpec(memory_space=pltpu.VMEM)] * (total - smem)
    return pl.pallas_call(
        kernel,
        out_shape=[jax.ShapeDtypeStruct(shape, kind) for shape, kind in outs],
        in_specs=spaces,
        out_specs=[pl.BlockSpec(memory_space=pltpu.VMEM)] * len(outs),
        scratch_shapes=[pltpu.VMEM(shape, kind) for shape, kind in scratch],
        compiler_params=pltpu.CompilerParams(vmem_limit_bytes=24 * 2**20),
        cost_estimate=pl.CostEstimate(flops=flops, bytes_accessed=size, transcendentals=0),
    )


def selector(owner):
    row, lane = iota((512, 128), 0), iota((512, 128), 1)
    slot = (((row >> 4) & 3) * 2 + ((row >> 1) & 1)) * 8 + (row >> 6)
    hit = (owner == slot) & ((lane & 1) == (row & 1))
    pair = (row >> 2) & 3
    return jnp.concatenate([one_hot(hit & (pair == q)) for q in range(4)], axis=1)


def pack(field, owner):
    wide = jnp.concatenate([field(q) for q in range(4)], axis=1)
    high, low = split(wide)
    chosen = selector(owner)
    return dot_nt(chosen, high) + dot_nt(chosen, low)


def unpack(rows, owner):
    high, low = split(rows)
    chosen = selector(owner)
    return dot_tn(high, chosen) + dot_tn(low, chosen)


def begin_kernel(owner, static_in, packed, work):
    for lon in range(8):
        work[lon] = static_in[pl.ds(lon, 64, stride=8), :]
    packed[...] = pack(lambda q: work[2 * q : 2 * q + 2].reshape(128, 128), owner[...])


def begin_members_kernel(ens_in, perts_in, classes, up, down, ens, perts, flat):
    flat[...] = perts_in[...].astype(f32).reshape(1024, 128)
    for lon in range(8):
        member = ens_in[pl.ds(lon, 64, stride=8), :]
        ens[lon] = member
        perts[lon] = flat[pl.ds(lon, 128, stride=8), :]
        target, place = (down, lon) if lon < 4 else (up, lon - 4)
        target[place * 64 : place * 64 + 64] = member
    marks = classes[...].astype(f32)
    up[256:264] = marks
    down[256:264] = marks


def request_kernel(source_row, column_row, request, ranks):
    source = source_row[...]
    mine = iota((64, 512), 0) == source
    marks = one_hot(mine)
    earlier = one_hot(iota((512, 512), 0) < iota((512, 512), 1))
    count = dot_nn(marks, earlier)
    rank = jnp.sum(jnp.where(mine, count, 0.0), axis=0, keepdims=True).astype(i32)
    ranks[...] = rank
    wanted = column_row[...] + 1
    ranked = one_hot(iota((128, 512), 0) == rank)
    high = jnp.where(mine, (wanted >> 5).astype(f32), 0.0).astype(bf16)
    low = jnp.where(mine, (wanted & 31).astype(f32), 0.0).astype(bf16)
    request[...] = 32.0 * dot_nt(high, ranked) + dot_nt(low, ranked)


def slots_kernel(here, source_row, ranks, weight, innovation, first, second):
    z, level = here[0], here[1]
    source, rank = source_row[...], ranks[...]
    row = iota((256, 512), 0)
    place = ((row >> 7) & 1) * 16 + (row & 15)
    for j, target in enumerate((first, second)):
        tile = (2 * level + lax.rem(z + j, 2)) * 8 + ((row >> 4) & 7)
        mine = one_hot((source == tile) & (rank == place))
        for kind, values in enumerate((weight, innovation)):
            terms = split(values[...])
            target[kind * 256 : kind * 256 + 256] = dot_nt(mine, terms[0]) + dot_nt(mine, terms[1])


def load_matrices(here, first, second, matrices):
    z = here[0]
    for j, part in enumerate((first, second)):
        half = lax.rem(z + j, 2)
        for k in range(4):
            block = lax.bitwise_xor(lax.div(z, 2), k)
            rows = pl.ds(pl.multiple_of(block * 32, 32), 32)
            for var in range(2):
                start = k * 128 + var * 32
                matrices[half * 2 + var, rows, :] = part[start : start + 32]


def columns_of(rows):
    blocks = [
        jnp.concatenate([rows[u * 64 + l * 16 : u * 64 + l * 16 + 16] for u in range(8)], axis=0)
        for l in range(4)
    ]
    chunk = iota((128, 128), 1) >> 5
    out = []
    for c in range(4):
        joined = None
        for l in range(4):
            shift = (32 * (l - c)) % 128
            moved = pltpu.roll(blocks[l], shift, 1) if shift else blocks[l]
            joined = moved if l == 0 else jnp.where(chunk == l, moved, joined)
        out.append(joined)
    return out


def store_columns(out, columns, stride, offset):
    chunk = iota((128, 128), 1) >> 5
    for l in range(4):
        joined = None
        for c in range(4):
            shift = (32 * (c - l)) % 128
            moved = pltpu.roll(columns[c], shift, 1) if shift else columns[c]
            joined = moved if c == 0 else jnp.where(chunk == c, moved, joined)
        for u in range(8):
            start = (u * 4 + l) * stride + offset
            out[start : start + 16] = joined[u * 16 : u * 16 + 16]


def choose_half(product):
    half = (iota((256, 128), 0) >> 1) & 1
    return jnp.where(half == 0, product[:, :128], product[:, 128:])


def forward_columns(columns, matrices):
    out = [None] * 4
    for var in range(2):
        stacked = jnp.concatenate([columns[var], columns[2 + var]], axis=0)
        pair = jnp.concatenate([matrices[var], matrices[2 + var]], axis=0)
        chosen = choose_half(three(dot_nt, stacked, pair))
        out[var], out[2 + var] = chosen[:128], chosen[128:]
    return out


def backward_columns(columns, matrices):
    out = [None] * 4
    for var in range(2):
        stacked = jnp.concatenate([columns[var], columns[2 + var]], axis=0)
        pair = jnp.concatenate([matrices[var], matrices[2 + var]], axis=1)
        chosen = choose_half(three(dot_nn, stacked, pair))
        out[var], out[2 + var] = chosen[:128], chosen[128:]
    return out


def first_columns_kernel(here, rows, first, second, state, out, matrices):
    load_matrices(here, first, second, matrices)
    columns = columns_of(rows[...])
    for c in range(4):
        state[c] = columns[c]
    store_columns(out, forward_columns(columns, matrices), 16, 0)


def columns_kernel(last, here, rows, first, second, state, *refs):
    out, matrices = refs[-2], refs[-1]
    load_matrices(here, first, second, matrices)
    pulled = backward_columns(columns_of(rows[...]), matrices)
    columns = [(1.0 - step_length) * state[c] - step_length * pulled[c] for c in range(4)]
    forward = forward_columns(columns, matrices)
    if last:
        store_columns(out, forward, 32, 0)
        store_columns(out, columns, 32, 16)
    else:
        for c in range(4):
            refs[0][c] = columns[c]
        store_columns(out, forward, 16, 0)


def edges_kernel(owner, rows, low, high):
    wide = unpack(rows[...], owner[...])
    for lon in range(8):
        target, place = (low, lon) if lon < 4 else (high, lon - 4)
        q, side = lon // 2, lon % 2
        target[place] = wide[side * 64 : side * 64 + 64, q * 128 : q * 128 + 128]


def last_edges_kernel(owner, rows, low, high, final_static):
    both = rows[...]
    for kind in range(2):
        part = jnp.concatenate([both[p * 32 + kind * 16 : p * 32 + kind * 16 + 16] for p in range(32)], axis=0)
        wide = unpack(part, owner[...])
        for lon in range(8):
            q, side = lon // 2, lon % 2
            value = wide[side * 64 : side * 64 + 64, q * 128 : q * 128 + 128]
            if kind == 0:
                target, place = (low, lon) if lon < 4 else (high, lon - 4)
                target[place] = value
            else:
                final_static[pl.ds(lon, 64, stride=8), :] = value


def weights_kernel(scales, before, own, after, weights, kappa):
    marks = jnp.concatenate([before[...], own[...].astype(f32), after[...]], axis=0)
    lane = iota((16, 128), 1)
    for kind in range(2):
        value = jnp.zeros((24, 128), f32)
        for entry in range(8):
            value = jnp.where(marks == float(entry), scales[kind * 8 + entry], value)
        kappa[kind] = value
        centre = kappa[kind, 4:20]
        east = 0.5 * (centre + kappa[kind, 5:21])
        west = 0.5 * (kappa[kind, 3:19] + centre)
        north = jnp.where(lane < 127, 0.5 * (centre + pltpu.roll(centre, 127, 1)), 0.0)
        south = jnp.where(lane > 0, 0.5 * (centre + pltpu.roll(centre, 1, 1)), 0.0)
        weights[kind, 0] = east
        weights[kind, 1] = west
        weights[kind, 2] = north
        weights[kind, 3] = south
        weights[kind, 4] = 1.0 / (1.0 + east + west + north + south)


def neighbours(field, i, weight):
    return (
        weight(0, i) * field[i + 1]
        + weight(1, i) * field[i - 1]
        + weight(2, i) * pltpu.roll(field[i], 127, 1)
        + weight(3, i) * pltpu.roll(field[i], 1, 1)
    )


def diffuse(source, weight):
    current = dict(enumerate(source))
    for sweep in range(NSWEEP):
        current = {
            i: weight(4, i) * (source[i] + neighbours(current, i, weight))
            for i in range(sweep + 1, 15 - sweep)
        }
    return current


def diffuse_transposed(source, weight):
    carried = dict(enumerate(source))
    total = None
    for sweep in range(NSWEEP):
        scaled = {i: weight(4, i) * carried[i] for i in range(sweep, 16 - sweep)}
        total = {i: scaled[i] if total is None else total[i] + scaled[i] for i in range(4, 12)}
        carried = {i: neighbours(scaled, i, weight) for i in range(sweep + 1, 15 - sweep)}
    return {i: total[i] + carried[i] for i in range(4, 12)}


def weight_of(weights, kind):
    return lambda which, i: weights[kind, which, i : i + 1, :]


def wide_loader(before, low, high, after):
    parts = (before, low, high, after)
    return lambda rows: [parts[i // 4][i % 4, rows, :] for i in range(16)]


def members_kernel(ens, ens_before, ens_after, perts, weights, out):

    def ens_at(rows):
        return (
            [ens_before[pl.ds(i * 64 + rows, 8), :] for i in range(4)]
            + [ens[i, pl.ds(rows, 8), :] for i in range(8)]
            + [ens_after[pl.ds(i * 64 + rows, 8), :] for i in range(4)]
        )

    def levels(step, carry):
        base = pl.multiple_of(step * 8, 8)
        members = [diffuse(ens_at(e * 32 + base), weight_of(weights, 1)) for e in range(2)]
        for var in range(2):
            for lon in range(8):
                total = sum(
                    perts[lon, pl.ds((e * 2 + var) * 32 + base, 8), :] * members[e][lon + 4] for e in range(2)
                )
                out[lon, pl.ds(var * 32 + base, 8), :] = beta_ensemble * total
        return carry

    lax.fori_loop(0, 4, levels, 0)


def increments(loader, members, weights, target):

    def levels(step, carry):
        for var in range(2):
            rows = pl.ds(pl.multiple_of(var * 32 + step * 8, 8), 8)
            smooth = diffuse(loader(rows), weight_of(weights, 0))
            for lon in range(8):
                target[lon, rows, :] = beta_static * smooth[lon + 4] + members[lon, rows, :]
        return carry

    lax.fori_loop(0, 4, levels, 0)


def slot_columns(high, low, start, count, half):
    row = iota((count, 64), 0) + start
    tile = ((row >> 4) & 7) * 8 + (row >> 7)
    repeat = one_hot(tile == iota((count, 64), 1))
    spread = 32.0 * dot_nn(repeat, high) + dot_nn(repeat, low)
    place = (iota((count, 128), 0) & 15) + half * 16
    return jnp.sum(jnp.where(iota((count, 128), 1) == place, spread, 0.0), axis=1, keepdims=True).astype(i32) - 1


def observe_kernel(request, low, high, before, after, members, weights, out, field, terms):
    increments(wide_loader(before, low, high, after), members, weights, field)
    for q in range(4):
        pair = jnp.concatenate([field[2 * q], field[2 * q + 1]], axis=1)
        terms[q] = jnp.concatenate(split(pair), axis=0)
    wanted = request[...].astype(i32)
    first, second = (wanted >> 5).astype(f32).astype(bf16), (wanted & 31).astype(f32).astype(bf16)
    wide = iota((512, 256), 1)

    def block(step, carry):
        start = pl.multiple_of(step * 512, 512)
        sums = []
        for half in range(2):
            column = slot_columns(first, second, start, 512, half)
            total = sum(dot_nt(one_hot(column - q * 256 == wide), terms[q]) for q in range(4))
            sums.append(total + pltpu.roll(total, 64, 1))
        out[pl.ds(start, 512), :] = jnp.where(iota((512, 128), 1) < 64, sums[0], sums[1])
        return carry

    lax.fori_loop(0, 2, block, 0)


def last_kernel(low, high, before, after, members, weights, ens, out, final_ens, field):
    increments(wide_loader(before, low, high, after), members, weights, field)
    for lon in range(8):
        out[pl.ds(lon, 64, stride=8), :] = field[lon]
        final_ens[pl.ds(lon, 64, stride=8), :] = ens[lon]


def operators_kernel(here, arrived, first, second, first_slots, second_slots, out, stacked):
    z = here[0]
    lane = iota((128, 128), 1) < 64

    def start(u, k, half):
        level = lax.bitwise_xor(lax.div(z, 2), k)
        return pl.ds(pl.multiple_of((u * 4 + level) * 32 + half * 16, 16), 16)

    for j, (part, slots) in enumerate(((first, first_slots), (second, second_slots))):
        half = lax.rem(z + j, 2)
        blocks = [
            jnp.concatenate([arrived[start(u, k, half), :] for u in range(8)], axis=0) for k in range(4)
        ]
        operator = jnp.concatenate([part[k * 128 + 64 : k * 128 + 128] for k in range(4)], axis=0)
        for pair in range(2):
            even, odd = blocks[2 * pair], blocks[2 * pair + 1]
            lanes = slice(pair * 128, pair * 128 + 128)
            stacked[0:128, lanes] = jnp.where(lane, even, pltpu.roll(odd, 64, 1))
            stacked[128:256, lanes] = jnp.where(lane, pltpu.roll(even, 64, 1), odd)
        observed = three(dot_nn, stacked[...], operator)
        departure = slots[0:256] * (observed - slots[256:512])
        pulled = three(dot_nt, departure, operator)
        for pair in range(2):
            lanes = slice(pair * 128, pair * 128 + 128)
            upper, lower = pulled[:128, lanes], pulled[128:, lanes]
            values = (
                jnp.where(lane, upper, pltpu.roll(lower, 64, 1)),
                jnp.where(lane, pltpu.roll(upper, 64, 1), lower),
            )
            for side in range(2):
                for u in range(8):
                    out[start(u, 2 * pair + side, half), :] = values[side][u * 16 : u * 16 + 16]


def collect_kernel(request, arrived, perts, low, high, turned):
    value = arrived[...]
    first = value.astype(bf16).astype(f32)
    rest = value - first
    lane = iota((1024, 128), 1) < 64
    stacked = jnp.concatenate(
        [
            jnp.where(lane, first, pltpu.roll(rest, 64, 1)),
            jnp.where(lane, pltpu.roll(first, 64, 1), rest),
        ],
        axis=0,
    )
    turned[...] = stacked.T.astype(bf16)
    wanted = request[...].astype(i32)
    upper, lower = (wanted >> 5).astype(f32).astype(bf16), (wanted & 31).astype(f32).astype(bf16)
    columns = [slot_columns(upper, lower, 0, 1024, half) for half in range(2)]
    wide = iota((1024, 256), 1)
    for q in range(4):
        hits = jnp.concatenate([one_hot(columns[half] - q * 256 == wide) for half in range(2)], axis=0)
        both = dot_nn(turned[...], hits)
        total = both[:64] + both[64:]
        target = low if q < 2 else high
        for side in range(2):
            place = (q % 2) * 2 + side
            gradient = total[:, side * 128 : side * 128 + 128]
            target[place, 0:64] = gradient
            factor = perts[2 * q + side]
            for e in range(2):
                mixed = factor[e * 64 : e * 64 + 32] * gradient[:32] + factor[e * 64 + 32 : e * 64 + 64] * gradient[32:]
                target[place, 64 + e * 32 : 96 + e * 32] = beta_ensemble * mixed


def pull_kernel(owner, low, high, before, after, weights, packed, field):
    loader = wide_loader(before, low, high, after)

    def levels(step, carry):
        for var in range(2):
            rows = pl.ds(pl.multiple_of(var * 32 + step * 8, 8), 8)
            smooth = diffuse_transposed([beta_static * value for value in loader(rows)], weight_of(weights, 0))
            for lon in range(8):
                field[lon, rows, :] = smooth[lon + 4]
        return carry

    lax.fori_loop(0, 4, levels, 0)
    packed[...] = pack(lambda q: field[2 * q : 2 * q + 2].reshape(128, 128), owner[...])


def pull_members_kernel(low, high, before, after, ens, weights, new_ens, new_low, new_high):
    loader = wide_loader(before, low, high, after)

    def levels(step, carry):
        for e in range(2):
            base = pl.multiple_of(e * 32 + step * 8, 8)
            smooth = diffuse_transposed(loader(pl.ds(64 + base, 8)), weight_of(weights, 1))
            for lon in range(8):
                value = (1.0 - step_length) * ens[lon, pl.ds(base, 8), :] - step_length * smooth[lon + 4]
                new_ens[lon, pl.ds(base, 8), :] = value
                if lon < 4:
                    new_low[pl.ds(lon * 64 + base, 8), :] = value
                else:
                    new_high[pl.ds((lon - 4) * 64 + base, 8), :] = value
        return carry

    lax.fori_loop(0, 4, levels, 0)


def on_device(
    control_static,
    control_ens,
    ens_perts,
    band_sqrt,
    band_owner,
    scale_class,
    static_scales,
    local_scales,
    obs_source,
    obs_column,
    obs_jac,
    innovation,
    obs_weight,
):
    tiles = 64
    upward = [(i, (i + 1) % tiles) for i in range(tiles)]
    downward = [(i, (i - 1) % tiles) for i in range(tiles)]

    def to_plane(value):
        return lax.all_to_all(value, PLANE, 0, 0, tiled=True)

    here = jnp.stack([lax.axis_index("z"), lax.axis_index("yh") * 2 + lax.axis_index("core")]).astype(i32)
    scales = jnp.concatenate([static_scales, local_scales])
    owner = jnp.repeat(band_owner, 2).reshape(1, 128)

    shared = jnp.concatenate(
        [band_sqrt.reshape(64, 128), jnp.transpose(obs_jac, (0, 2, 3, 1)).reshape(64, 128)], axis=0
    )
    swap = [(0, 1), (1, 0)]
    shared = jnp.concatenate([shared, lax.ppermute(shared, "core", swap)], axis=0)
    shared = jnp.concatenate([shared, lax.ppermute(shared, "yh", swap)], axis=0)
    exchange = [(z * 4 + l, (2 * l + (j + z) % 2) * 4 + z // 2) for j in range(2) for z in range(8) for l in range(4)]

    def spread(value, j):
        return lax.ppermute(value, ("z",) + LEV, exchange[j * 32 : j * 32 + 32])

    matrices = [spread(shared, j) for j in range(2)]
    (packed,) = call(begin_kernel, [((512, 128), f32)], [((8, 64, 128), f32)], total=2)(
        owner, control_static.reshape(512, 128)
    )
    arrived = to_plane(packed)
    source_row = obs_source.reshape(1, 512)
    request, ranks = call(request_kernel, [((64, 128), f32), ((1, 512), i32)], total=2)(
        source_row, obs_column.reshape(1, 512)
    )
    request, arrived = lax.optimization_barrier((request, arrived))
    wanted = lax.all_to_all(request, TILE, 0, 0, tiled=True)
    arrived, wanted, control_ens, ranks = lax.optimization_barrier((arrived, wanted, control_ens, ranks))
    slots = call(slots_kernel, [((512, 128), f32), ((512, 128), f32)], smem=1, total=5)(
        here, source_row, ranks, obs_weight, innovation
    )
    slots = [spread(slots[j], j) for j in range(2)]

    send_up, send_down, ens, perts = call(
        begin_members_kernel,
        [((264, 128), f32), ((264, 128), f32), ((8, 64, 128), f32), ((8, 128, 128), f32)],
        [((1024, 128), f32)],
        total=3,
    )(control_ens.reshape(512, 128), ens_perts.reshape(128, 8, 128), scale_class)
    from_before = lax.ppermute(send_up, TILE, upward)
    from_after = lax.ppermute(send_down, TILE, downward)
    ens_before, marks_before = from_before[:256], from_before[256:]
    ens_after, marks_after = from_after[:256], from_after[256:]

    state, out = call(
        first_columns_kernel,
        [((4, 128, 128), f32), ((512, 128), f32)],
        [((4, 128, 128), f32)],
        smem=1,
        total=4,
    )(here, arrived, *matrices)

    (faces,) = call(weights_kernel, [((2, 5, 16, 128), f32)], [((2, 24, 128), f32)], smem=1, total=4)(
        scales, marks_before, scale_class, marks_after
    )

    half_shape = ((4, 64, 128), f32)
    mixed_shape = ((4, 128, 128), f32)
    scratch = ((8, 64, 128), f32)

    def halos(low, high):
        return lax.ppermute(high, TILE, upward), lax.ppermute(low, TILE, downward)

    def members_of(ens, ens_before, ens_after):
        return call(members_kernel, [((8, 64, 128), f32)], total=5)(ens, ens_before, ens_after, perts, faces)[0]

    for iteration in range(ITERS):
        low, high = call(edges_kernel, [half_shape, half_shape], total=2)(owner, to_plane(out))
        before, after = halos(low, high)
        members = members_of(ens, ens_before, ens_after)
        (outgoing,) = call(
            observe_kernel, [((1024, 128), f32)], [scratch, ((4, 128, 256), bf16)], total=7
        )(wanted, low, high, before, after, members, faces)
        (returned,) = call(operators_kernel, [((1024, 128), f32)], [((256, 256), f32)], smem=1, total=6)(
            here, to_plane(outgoing), *matrices, *slots
        )
        low, high = call(collect_kernel, [mixed_shape, mixed_shape], [((128, 2048), bf16)], total=3)(
            wanted, to_plane(returned), perts
        )
        before, after = halos(low, high)
        (packed,) = call(pull_kernel, [((512, 128), f32)], [scratch], total=6)(owner, low, high, before, after, faces)
        ens, ens_low, ens_high = call(
            pull_members_kernel, [((8, 64, 128), f32), ((256, 128), f32), ((256, 128), f32)], total=6
        )(low, high, before, after, ens, faces)
        ens_before = lax.ppermute(ens_high, TILE, upward)
        ens_after = lax.ppermute(ens_low, TILE, downward)
        last = iteration == ITERS - 1
        results = call(
            functools.partial(columns_kernel, last),
            [((1024, 128), f32)] if last else [((4, 128, 128), f32), ((512, 128), f32)],
            [((4, 128, 128), f32)],
            smem=1,
            total=5,
        )(here, to_plane(packed), *matrices, state)
        if not last:
            state = results[0]
        out = results[-1]

    low, high, final_static = call(last_edges_kernel, [half_shape, half_shape, ((512, 128), f32)], total=2)(
        owner, to_plane(out)
    )
    before, after = halos(low, high)
    members = members_of(ens, ens_before, ens_after)
    analysis, final_ens = call(last_kernel, [((512, 128), f32), ((512, 128), f32)], [scratch], total=7)(
        low, high, before, after, members, faces, ens
    )
    return tuple(value.reshape(2, 32, 8, 128) for value in (analysis, final_static, final_ens))


def solution(mesh):
    physical = Mesh(mesh.devices.reshape(8, 2, 4, 2, 2), AXES)
    return jax.shard_map(
        on_device,
        mesh=physical,
        in_specs=(
            P(None, LEV, TILE, None),
            P(None, LEV, TILE, None),
            P(None, None, LEV, TILE, None),
            P(TILE, None, LEV, None),
            P(),
            P(TILE, None),
            P(),
            P(),
            P(TILE, None),
            P(TILE),
            P(TILE, None, None, LEV),
            P(None, TILE),
            P(None, TILE),
        ),
        out_specs=(
            P(None, LEV, TILE, None),
            P(None, LEV, TILE, None),
            P(None, LEV, TILE, None),
        ),
        check_vma=False,
    )
```

```python
import functools

import jax
import jax.numpy as jnp
from jax import lax
from jax.experimental import pallas as pl
from jax.experimental.pallas import tpu as pltpu
from jax.sharding import Mesh, PartitionSpec as P

NSWEEP = 4
ITERS = 2

beta_static = 0.8
beta_ensemble = 0.6
step_length = 0.3

LEV = ("yh", "core")
TILE = ("z", "yl", "x")
PLANE = ("yl", "x", "yh", "core")
AXES = ("z", "yl", "x", "yh", "core")

f32, bf16, i32 = jnp.float32, jnp.bfloat16, jnp.int32


def iota(shape, dim):
    return lax.broadcasted_iota(i32, shape, dim)


def split(value):
    high = value.astype(bf16)
    return high, (value - high.astype(f32)).astype(bf16)


def dot_nn(a, b):
    return lax.dot_general(a, b, (((1,), (0,)), ((), ())), preferred_element_type=f32)


def dot_nt(a, b):
    return lax.dot_general(a, b, (((1,), (1,)), ((), ())), preferred_element_type=f32)


def dot_tn(a, b):
    return lax.dot_general(a, b, (((0,), (0,)), ((), ())), preferred_element_type=f32)


def three(dot, a, b):
    (ah, al), (bh, bl) = split(a), split(b)
    return dot(ah, bh) + (dot(ah, bl) + dot(al, bh))


def one_hot(mask):
    return jnp.where(mask, 1.0, 0.0).astype(bf16)


def call(kernel, outs, scratch=(), smem=0, total=0, flops=10**8, size=6 * 10**6):
    spaces = [pl.BlockSpec(memory_space=pltpu.SMEM)] * smem
    spaces += [pl.BlockSpec(memory_space=pltpu.VMEM)] * (total - smem)
    return pl.pallas_call(
        kernel,
        out_shape=[jax.ShapeDtypeStruct(shape, kind) for shape, kind in outs],
        in_specs=spaces,
        out_specs=[pl.BlockSpec(memory_space=pltpu.VMEM)] * len(outs),
        scratch_shapes=[pltpu.VMEM(shape, kind) for shape, kind in scratch],
        compiler_params=pltpu.CompilerParams(vmem_limit_bytes=24 * 2**20),
        cost_estimate=pl.CostEstimate(flops=flops, bytes_accessed=size, transcendentals=0),
    )


def selector(owner):
    row, lane = iota((512, 128), 0), iota((512, 128), 1)
    slot = (((row >> 4) & 3) * 2 + ((row >> 1) & 1)) * 8 + (row >> 6)
    hit = (owner == slot) & ((lane & 1) == (row & 1))
    pair = (row >> 2) & 3
    return jnp.concatenate([one_hot(hit & (pair == q)) for q in range(4)], axis=1)


def pack(field, owner):
    wide = jnp.concatenate([field(q) for q in range(4)], axis=1)
    high, low = split(wide)
    chosen = selector(owner)
    return dot_nt(chosen, high) + dot_nt(chosen, low)


def unpack(rows, owner):
    high, low = split(rows)
    chosen = selector(owner)
    return dot_tn(high, chosen) + dot_tn(low, chosen)


def begin_kernel(owner, static_in, packed, work):
    for lon in range(8):
        work[lon] = static_in[pl.ds(lon, 64, stride=8), :]
    packed[...] = pack(lambda q: work[2 * q : 2 * q + 2].reshape(128, 128), owner[...])


def begin_members_kernel(ens_in, perts_in, classes, up, down, ens, perts, flat):
    flat[...] = perts_in[...].astype(f32).reshape(1024, 128)
    for lon in range(8):
        member = ens_in[pl.ds(lon, 64, stride=8), :]
        ens[lon] = member
        perts[lon] = flat[pl.ds(lon, 128, stride=8), :]
        target, place = (down, lon) if lon < 4 else (up, lon - 4)
        target[place * 64 : place * 64 + 64] = member
    marks = classes[...].astype(f32)
    up[256:264] = marks
    down[256:264] = marks


def request_kernel(source_row, column_row, request, ranks):
    source = source_row[...]
    mine = iota((64, 512), 0) == source
    marks = one_hot(mine)
    earlier = one_hot(iota((512, 512), 0) < iota((512, 512), 1))
    count = dot_nn(marks, earlier)
    rank = jnp.sum(jnp.where(mine, count, 0.0), axis=0, keepdims=True).astype(i32)
    ranks[...] = rank
    wanted = column_row[...] + 1
    ranked = one_hot(iota((128, 512), 0) == rank)
    high = jnp.where(mine, (wanted >> 5).astype(f32), 0.0).astype(bf16)
    low = jnp.where(mine, (wanted & 31).astype(f32), 0.0).astype(bf16)
    request[...] = 32.0 * dot_nt(high, ranked) + dot_nt(low, ranked)


def slots_kernel(here, source_row, ranks, weight, innovation, shared, first, second):
    z, level = here[0], here[1]
    source, rank = source_row[...], ranks[...]
    row = iota((256, 512), 0)
    place = ((row >> 7) & 1) * 16 + (row & 15)
    for j, target in enumerate((first, second)):
        for k in range(4):
            target[k * 64 : k * 64 + 64] = shared[k * 128 + 64 : k * 128 + 128]
        tile = lax.rem(z + level + 4 * j + 3 * lax.rem(z, 2), 8) * 8 + ((row >> 4) & 7)
        mine = one_hot((source == tile) & (rank == place))
        for kind, values in enumerate((weight, innovation)):
            terms = split(values[...])
            target[256 + kind * 256 : 512 + kind * 256] = dot_nt(mine, terms[0]) + dot_nt(mine, terms[1])


def load_matrices(here, first, second, matrices):
    turn = lax.rem(here[0] - 2 * here[1] + 8, 8)
    for j, part in enumerate((first, second)):
        half = lax.bitwise_xor(lax.div(turn, 4), j)
        for k in range(4):
            block = lax.bitwise_xor(lax.rem(turn, 4), k)
            rows = pl.ds(pl.multiple_of(block * 32, 32), 32)
            for var in range(2):
                start = k * 64 + var * 32
                matrices[half * 2 + var, rows, :] = part[start : start + 32]


def columns_of(rows):
    blocks = [
        jnp.concatenate([rows[u * 64 + l * 16 : u * 64 + l * 16 + 16] for u in range(8)], axis=0)
        for l in range(4)
    ]
    chunk = iota((128, 128), 1) >> 5
    out = []
    for c in range(4):
        joined = None
        for l in range(4):
            shift = (32 * (l - c)) % 128
            moved = pltpu.roll(blocks[l], shift, 1) if shift else blocks[l]
            joined = moved if l == 0 else jnp.where(chunk == l, moved, joined)
        out.append(joined)
    return out


def store_columns(out, columns, stride, offset):
    chunk = iota((128, 128), 1) >> 5
    for l in range(4):
        joined = None
        for c in range(4):
            shift = (32 * (c - l)) % 128
            moved = pltpu.roll(columns[c], shift, 1) if shift else columns[c]
            joined = moved if c == 0 else jnp.where(chunk == c, moved, joined)
        for u in range(8):
            start = (u * 4 + l) * stride + offset
            out[start : start + 16] = joined[u * 16 : u * 16 + 16]


def choose_half(product):
    half = (iota((256, 128), 0) >> 1) & 1
    return jnp.where(half == 0, product[:, :128], product[:, 128:])


def forward_columns(columns, matrices):
    out = [None] * 4
    for var in range(2):
        stacked = jnp.concatenate([columns[var], columns[2 + var]], axis=0)
        pair = jnp.concatenate([matrices[var], matrices[2 + var]], axis=0)
        chosen = choose_half(three(dot_nt, stacked, pair))
        out[var], out[2 + var] = chosen[:128], chosen[128:]
    return out


def backward_columns(columns, matrices):
    out = [None] * 4
    for var in range(2):
        stacked = jnp.concatenate([columns[var], columns[2 + var]], axis=0)
        pair = jnp.concatenate([matrices[var], matrices[2 + var]], axis=1)
        chosen = choose_half(three(dot_nn, stacked, pair))
        out[var], out[2 + var] = chosen[:128], chosen[128:]
    return out


def first_columns_kernel(here, rows, first, second, state, out, matrices):
    load_matrices(here, first, second, matrices)
    columns = columns_of(rows[...])
    for c in range(4):
        state[c] = columns[c]
    store_columns(out, forward_columns(columns, matrices), 16, 0)


def columns_kernel(last, here, rows, first, second, state, *refs):
    out, matrices = refs[-2], refs[-1]
    load_matrices(here, first, second, matrices)
    pulled = backward_columns(columns_of(rows[...]), matrices)
    columns = [(1.0 - step_length) * state[c] - step_length * pulled[c] for c in range(4)]
    forward = forward_columns(columns, matrices)
    if last:
        store_columns(out, forward, 32, 0)
        store_columns(out, columns, 32, 16)
    else:
        for c in range(4):
            refs[0][c] = columns[c]
        store_columns(out, forward, 16, 0)


def edges_kernel(owner, rows, low, high):
    wide = unpack(rows[...], owner[...])
    for lon in range(8):
        target, place = (low, lon) if lon < 4 else (high, lon - 4)
        q, side = lon // 2, lon % 2
        target[place] = wide[side * 64 : side * 64 + 64, q * 128 : q * 128 + 128]


def last_edges_kernel(owner, rows, low, high, final_static):
    both = rows[...]
    for kind in range(2):
        part = jnp.concatenate([both[p * 32 + kind * 16 : p * 32 + kind * 16 + 16] for p in range(32)], axis=0)
        wide = unpack(part, owner[...])
        for lon in range(8):
            q, side = lon // 2, lon % 2
            value = wide[side * 64 : side * 64 + 64, q * 128 : q * 128 + 128]
            if kind == 0:
                target, place = (low, lon) if lon < 4 else (high, lon - 4)
                target[place] = value
            else:
                final_static[pl.ds(lon, 64, stride=8), :] = value


def weights_kernel(scales, before, own, after, weights, kappa):
    marks = jnp.concatenate([before[...], own[...].astype(f32), after[...]], axis=0)
    lane = iota((16, 128), 1)
    for kind in range(2):
        value = jnp.zeros((24, 128), f32)
        for entry in range(8):
            value = jnp.where(marks == float(entry), scales[kind * 8 + entry], value)
        kappa[kind] = value
        centre = kappa[kind, 4:20]
        east = 0.5 * (centre + kappa[kind, 5:21])
        west = 0.5 * (kappa[kind, 3:19] + centre)
        north = jnp.where(lane < 127, 0.5 * (centre + pltpu.roll(centre, 127, 1)), 0.0)
        south = jnp.where(lane > 0, 0.5 * (centre + pltpu.roll(centre, 1, 1)), 0.0)
        weights[kind, 0] = east
        weights[kind, 1] = west
        weights[kind, 2] = north
        weights[kind, 3] = south
        weights[kind, 4] = 1.0 / (1.0 + east + west + north + south)


def neighbours(field, i, weight):
    return (
        weight(0, i) * field[i + 1]
        + weight(1, i) * field[i - 1]
        + weight(2, i) * pltpu.roll(field[i], 127, 1)
        + weight(3, i) * pltpu.roll(field[i], 1, 1)
    )


def diffuse(source, weight):
    current = dict(enumerate(source))
    for sweep in range(NSWEEP):
        current = {
            i: weight(4, i) * (source[i] + neighbours(current, i, weight))
            for i in range(sweep + 1, 15 - sweep)
        }
    return current


def diffuse_transposed(source, weight):
    carried = dict(enumerate(source))
    total = None
    for sweep in range(NSWEEP):
        scaled = {i: weight(4, i) * carried[i] for i in range(sweep, 16 - sweep)}
        total = {i: scaled[i] if total is None else total[i] + scaled[i] for i in range(4, 12)}
        carried = {i: neighbours(scaled, i, weight) for i in range(sweep + 1, 15 - sweep)}
    return {i: total[i] + carried[i] for i in range(4, 12)}


def weight_of(weights, kind):
    return lambda which, i: weights[kind, which, i : i + 1, :]


def wide_loader(before, low, high, after):
    parts = (before, low, high, after)
    return lambda rows: [parts[i // 4][i % 4, rows, :] for i in range(16)]


def members_kernel(ens, ens_before, ens_after, perts, weights, out):

    def ens_at(rows):
        return (
            [ens_before[pl.ds(i * 64 + rows, 8), :] for i in range(4)]
            + [ens[i, pl.ds(rows, 8), :] for i in range(8)]
            + [ens_after[pl.ds(i * 64 + rows, 8), :] for i in range(4)]
        )

    def levels(step, carry):
        base = pl.multiple_of(step * 8, 8)
        members = [diffuse(ens_at(e * 32 + base), weight_of(weights, 1)) for e in range(2)]
        for var in range(2):
            for lon in range(8):
                total = sum(
                    perts[lon, pl.ds((e * 2 + var) * 32 + base, 8), :] * members[e][lon + 4] for e in range(2)
                )
                out[lon, pl.ds(var * 32 + base, 8), :] = beta_ensemble * total
        return carry

    lax.fori_loop(0, 4, levels, 0)


def increments(loader, members, weights, target):

    def levels(step, carry):
        for var in range(2):
            rows = pl.ds(pl.multiple_of(var * 32 + step * 8, 8), 8)
            smooth = diffuse(loader(rows), weight_of(weights, 0))
            for lon in range(8):
                target[lon, rows, :] = beta_static * smooth[lon + 4] + members[lon, rows, :]
        return carry

    lax.fori_loop(0, 4, levels, 0)


def slot_columns(high, low, start, count, half):
    row = iota((count, 64), 0) + start
    tile = ((row >> 4) & 7) * 8 + (row >> 7)
    repeat = one_hot(tile == iota((count, 64), 1))
    spread = 32.0 * dot_nn(repeat, high) + dot_nn(repeat, low)
    place = (iota((count, 128), 0) & 15) + half * 16
    return jnp.sum(jnp.where(iota((count, 128), 1) == place, spread, 0.0), axis=1, keepdims=True).astype(i32) - 1


def observe_kernel(request, low, high, before, after, members, weights, out, field, terms):
    increments(wide_loader(before, low, high, after), members, weights, field)
    for q in range(4):
        pair = jnp.concatenate([field[2 * q], field[2 * q + 1]], axis=1)
        terms[q] = jnp.concatenate(split(pair), axis=0)
    wanted = request[...].astype(i32)
    first, second = (wanted >> 5).astype(f32).astype(bf16), (wanted & 31).astype(f32).astype(bf16)
    wide = iota((256, 256), 1)

    def block(step, carry):
        start = pl.multiple_of(step * 256, 256)
        sums = []
        for half in range(2):
            column = slot_columns(first, second, start, 256, half)
            total = sum(dot_nt(one_hot(column - q * 256 == wide), terms[q]) for q in range(4))
            sums.append(total + pltpu.roll(total, 64, 1))
        out[pl.ds(start, 256), :] = jnp.where(iota((256, 128), 1) < 64, sums[0], sums[1])
        return carry

    lax.fori_loop(0, 4, block, 0)


def last_kernel(low, high, before, after, members, weights, ens, out, final_ens, field):
    increments(wide_loader(before, low, high, after), members, weights, field)
    for lon in range(8):
        out[pl.ds(lon, 64, stride=8), :] = field[lon]
        final_ens[pl.ds(lon, 64, stride=8), :] = ens[lon]


def operators_kernel(here, arrived, first, second, out, stacked):
    turn = lax.rem(here[0] - 2 * here[1] + 8, 8)
    lane = iota((128, 128), 1) < 64

    def start(u, k, half):
        level = lax.bitwise_xor(lax.rem(turn, 4), k)
        return pl.ds(pl.multiple_of((u * 4 + level) * 32 + half * 16, 16), 16)

    for j, part in enumerate((first, second)):
        half = lax.bitwise_xor(lax.div(turn, 4), j)
        blocks = [
            jnp.concatenate([arrived[start(u, k, half), :] for u in range(8)], axis=0) for k in range(4)
        ]
        operator = part[0:256]
        for pair in range(2):
            even, odd = blocks[2 * pair], blocks[2 * pair + 1]
            lanes = slice(pair * 128, pair * 128 + 128)
            stacked[0:128, lanes] = jnp.where(lane, even, pltpu.roll(odd, 64, 1))
            stacked[128:256, lanes] = jnp.where(lane, pltpu.roll(even, 64, 1), odd)
        observed = three(dot_nn, stacked[...], operator)
        departure = part[256:512] * (observed - part[512:768])
        pulled = three(dot_nt, departure, operator)
        for pair in range(2):
            lanes = slice(pair * 128, pair * 128 + 128)
            upper, lower = pulled[:128, lanes], pulled[128:, lanes]
            values = (
                jnp.where(lane, upper, pltpu.roll(lower, 64, 1)),
                jnp.where(lane, pltpu.roll(upper, 64, 1), lower),
            )
            for side in range(2):
                for u in range(8):
                    out[start(u, 2 * pair + side, half), :] = values[side][u * 16 : u * 16 + 16]


def collect_kernel(request, arrived, perts, low, high, turned, places):
    value = arrived[...]
    first = value.astype(bf16).astype(f32)
    rest = value - first
    lane = iota((1024, 128), 1) < 64
    turned[:, 0:1024] = jnp.where(lane, first, pltpu.roll(rest, 64, 1)).T.astype(bf16)
    turned[:, 1024:2048] = jnp.where(lane, pltpu.roll(first, 64, 1), rest).T.astype(bf16)
    wanted = request[...].astype(i32)
    upper, lower = (wanted >> 5).astype(f32).astype(bf16), (wanted & 31).astype(f32).astype(bf16)
    for half in range(2):
        places[half * 1024 : half * 1024 + 1024] = jnp.broadcast_to(
            slot_columns(upper, lower, 0, 1024, half), (1024, 128)
        )

    def pair(q, carry):
        wide = iota((2048, 128), 1) + q * 256
        hits = jnp.concatenate([one_hot(places[...] == wide), one_hot(places[...] == wide + 128)], axis=1)
        both = dot_nn(turned[...], hits)
        total = both[:64] + both[64:]
        for side in range(2):
            gradient = total[:, side * 128 : side * 128 + 128]
            factor = perts[2 * q + side]
            mixed = [
                factor[e * 64 : e * 64 + 32] * gradient[:32] + factor[e * 64 + 32 : e * 64 + 64] * gradient[32:]
                for e in range(2)
            ]
            value = jnp.concatenate([gradient] + [beta_ensemble * part for part in mixed], axis=0)
            place = lax.rem(q, 2) * 2 + side

            @pl.when(q < 2)
            def _():
                low[place] = value

            @pl.when(q >= 2)
            def _():
                high[place] = value

        return carry

    lax.fori_loop(0, 4, pair, 0)


def pull_kernel(owner, low, high, before, after, weights, packed, field):
    loader = wide_loader(before, low, high, after)

    def levels(step, carry):
        for var in range(2):
            rows = pl.ds(pl.multiple_of(var * 32 + step * 8, 8), 8)
            smooth = diffuse_transposed([beta_static * value for value in loader(rows)], weight_of(weights, 0))
            for lon in range(8):
                field[lon, rows, :] = smooth[lon + 4]
        return carry

    lax.fori_loop(0, 4, levels, 0)
    packed[...] = pack(lambda q: field[2 * q : 2 * q + 2].reshape(128, 128), owner[...])


def pull_members_kernel(low, high, before, after, ens, weights, new_ens, new_low, new_high):
    loader = wide_loader(before, low, high, after)

    def levels(step, carry):
        for e in range(2):
            base = pl.multiple_of(e * 32 + step * 8, 8)
            smooth = diffuse_transposed(loader(pl.ds(64 + base, 8)), weight_of(weights, 1))
            for lon in range(8):
                value = (1.0 - step_length) * ens[lon, pl.ds(base, 8), :] - step_length * smooth[lon + 4]
                new_ens[lon, pl.ds(base, 8), :] = value
                if lon < 4:
                    new_low[pl.ds(lon * 64 + base, 8), :] = value
                else:
                    new_high[pl.ds((lon - 4) * 64 + base, 8), :] = value
        return carry

    lax.fori_loop(0, 4, levels, 0)


def on_device(
    control_static,
    control_ens,
    ens_perts,
    band_sqrt,
    band_owner,
    scale_class,
    static_scales,
    local_scales,
    obs_source,
    obs_column,
    obs_jac,
    innovation,
    obs_weight,
):
    tiles = 64
    upward = [(i, (i + 1) % tiles) for i in range(tiles)]
    downward = [(i, (i - 1) % tiles) for i in range(tiles)]

    def to_plane(value):
        return lax.all_to_all(value, PLANE, 0, 0, tiled=True)

    here = jnp.stack([lax.axis_index("z"), lax.axis_index("yh") * 2 + lax.axis_index("core")]).astype(i32)
    scales = jnp.concatenate([static_scales, local_scales])
    owner = jnp.repeat(band_owner, 2).reshape(1, 128)

    shared = jnp.concatenate(
        [band_sqrt.reshape(64, 128), jnp.transpose(obs_jac, (0, 2, 3, 1)).reshape(64, 128)], axis=0
    )
    swap = [(0, 1), (1, 0)]
    shared = jnp.concatenate([shared, lax.ppermute(shared, "core", swap)], axis=0)
    shared = jnp.concatenate([shared, lax.ppermute(shared, "yh", swap)], axis=0)
    exchange = [
        (z * 4 + l, (z + l + 4 * j + 3 * (z % 2)) % 8 * 4 + z // 2) for j in range(2) for z in range(8) for l in range(4)
    ]

    def spread(value, j):
        return lax.ppermute(value, ("z",) + LEV, exchange[j * 32 : j * 32 + 32])

    (packed,) = call(begin_kernel, [((512, 128), f32)], [((8, 64, 128), f32)], total=2)(
        owner, control_static.reshape(512, 128)
    )
    source_row = obs_source.reshape(1, 512)
    request, ranks = call(request_kernel, [((64, 128), f32), ((1, 512), i32)], total=2)(
        source_row, obs_column.reshape(1, 512)
    )
    matrices = shared.reshape(4, 128, 128)[:, :64].reshape(256, 128)
    matrices = [spread(matrices, j) for j in range(2)]
    request, arrived = lax.optimization_barrier((request, to_plane(packed)))
    wanted = lax.all_to_all(request, TILE, 0, 0, tiled=True)
    arrived, wanted, control_ens, ranks = lax.optimization_barrier((arrived, wanted, control_ens, ranks))
    parts = call(slots_kernel, [((768, 128), f32), ((768, 128), f32)], smem=1, total=6)(
        here, source_row, ranks, obs_weight, innovation, shared
    )
    parts, arrived = lax.optimization_barrier((parts, arrived))
    parts = [spread(parts[j], j) for j in range(2)]

    send_up, send_down, ens, perts = call(
        begin_members_kernel,
        [((264, 128), f32), ((264, 128), f32), ((8, 64, 128), f32), ((8, 128, 128), f32)],
        [((1024, 128), f32)],
        total=3,
    )(control_ens.reshape(512, 128), ens_perts.reshape(128, 8, 128), scale_class)
    from_before = lax.ppermute(send_up, TILE, upward)
    from_after = lax.ppermute(send_down, TILE, downward)
    ens_before, marks_before = from_before[:256], from_before[256:]
    ens_after, marks_after = from_after[:256], from_after[256:]

    state, out = call(
        first_columns_kernel,
        [((4, 128, 128), f32), ((512, 128), f32)],
        [((4, 128, 128), f32)],
        smem=1,
        total=4,
    )(here, arrived, *matrices)

    (faces,) = call(weights_kernel, [((2, 5, 16, 128), f32)], [((2, 24, 128), f32)], smem=1, total=4)(
        scales, marks_before, scale_class, marks_after
    )

    half_shape = ((4, 64, 128), f32)
    mixed_shape = ((4, 128, 128), f32)
    scratch = ((8, 64, 128), f32)

    def halos(low, high):
        return lax.ppermute(high, TILE, upward), lax.ppermute(low, TILE, downward)

    def members_of(ens, ens_before, ens_after):
        return call(members_kernel, [((8, 64, 128), f32)], total=5)(ens, ens_before, ens_after, perts, faces)[0]

    for iteration in range(ITERS):
        low, high = call(edges_kernel, [half_shape, half_shape], total=2)(owner, to_plane(out))
        before, after = halos(low, high)
        if iteration == 0:
            before, after, parts = lax.optimization_barrier((before, after, parts))
        members = members_of(ens, ens_before, ens_after)
        (outgoing,) = call(
            observe_kernel, [((1024, 128), f32)], [scratch, ((4, 128, 256), bf16)], total=7
        )(wanted, low, high, before, after, members, faces)
        (returned,) = call(operators_kernel, [((1024, 128), f32)], [((256, 256), f32)], smem=1, total=4)(
            here, to_plane(outgoing), *parts
        )
        low, high = call(collect_kernel, [mixed_shape, mixed_shape], [((128, 2048), bf16), ((2048, 128), i32)], total=3)(
            wanted, to_plane(returned), perts
        )
        before, after = halos(low, high)
        (packed,) = call(pull_kernel, [((512, 128), f32)], [scratch], total=6)(owner, low, high, before, after, faces)
        ens, ens_low, ens_high = call(
            pull_members_kernel, [((8, 64, 128), f32), ((256, 128), f32), ((256, 128), f32)], total=6
        )(low, high, before, after, ens, faces)
        ens_before = lax.ppermute(ens_high, TILE, upward)
        ens_after = lax.ppermute(ens_low, TILE, downward)
        last = iteration == ITERS - 1
        results = call(
            functools.partial(columns_kernel, last),
            [((1024, 128), f32)] if last else [((4, 128, 128), f32), ((512, 128), f32)],
            [((4, 128, 128), f32)],
            smem=1,
            total=5,
        )(here, to_plane(packed), *matrices, state)
        if not last:
            state = results[0]
        out = results[-1]

    low, high, final_static = call(last_edges_kernel, [half_shape, half_shape, ((512, 128), f32)], total=2)(
        owner, to_plane(out)
    )
    before, after = halos(low, high)
    members = members_of(ens, ens_before, ens_after)
    analysis, final_ens = call(last_kernel, [((512, 128), f32), ((512, 128), f32)], [scratch], total=7)(
        low, high, before, after, members, faces, ens
    )
    return tuple(value.reshape(2, 32, 8, 128) for value in (analysis, final_static, final_ens))


def solution(mesh):
    physical = Mesh(mesh.devices.reshape(8, 2, 4, 2, 2), AXES)
    return jax.shard_map(
        on_device,
        mesh=physical,
        in_specs=(
            P(None, LEV, TILE, None),
            P(None, LEV, TILE, None),
            P(None, None, LEV, TILE, None),
            P(TILE, None, LEV, None),
            P(),
            P(TILE, None),
            P(),
            P(),
            P(TILE, None),
            P(TILE),
            P(TILE, None, None, LEV),
            P(None, TILE),
            P(None, TILE),
        ),
        out_specs=(
            P(None, LEV, TILE, None),
            P(None, LEV, TILE, None),
            P(None, LEV, TILE, None),
        ),
        check_vma=False,
    )
```

```python
import functools

import jax
import jax.numpy as jnp
from jax import lax
from jax.experimental import pallas as pl
from jax.experimental.pallas import tpu as pltpu
from jax.sharding import Mesh, PartitionSpec as P

NSWEEP = 4
ITERS = 2

beta_static = 0.8
beta_ensemble = 0.6
step_length = 0.3

LEV = ("yh", "core")
TILE = ("z", "yl", "x")
PLANE = ("yl", "x", "yh", "core")
AXES = ("z", "yl", "x", "yh", "core")

f32, bf16, i32 = jnp.float32, jnp.bfloat16, jnp.int32


def iota(shape, dim):
    return lax.broadcasted_iota(i32, shape, dim)


def split(value):
    high = value.astype(bf16)
    return high, (value - high.astype(f32)).astype(bf16)


def dot_nn(a, b):
    return lax.dot_general(a, b, (((1,), (0,)), ((), ())), preferred_element_type=f32)


def dot_nt(a, b):
    return lax.dot_general(a, b, (((1,), (1,)), ((), ())), preferred_element_type=f32)


def dot_tn(a, b):
    return lax.dot_general(a, b, (((0,), (0,)), ((), ())), preferred_element_type=f32)


def three(dot, a, b):
    (ah, al), (bh, bl) = split(a), split(b)
    return dot(ah, bh) + (dot(ah, bl) + dot(al, bh))


def one_hot(mask):
    return jnp.where(mask, 1.0, 0.0).astype(bf16)


def call(kernel, outs, scratch=(), smem=0, total=0, flops=10**8, size=6 * 10**6):
    spaces = [pl.BlockSpec(memory_space=pltpu.SMEM)] * smem
    spaces += [pl.BlockSpec(memory_space=pltpu.VMEM)] * (total - smem)
    return pl.pallas_call(
        kernel,
        out_shape=[jax.ShapeDtypeStruct(shape, kind) for shape, kind in outs],
        in_specs=spaces,
        out_specs=[pl.BlockSpec(memory_space=pltpu.VMEM)] * len(outs),
        scratch_shapes=[pltpu.VMEM(shape, kind) for shape, kind in scratch],
        compiler_params=pltpu.CompilerParams(vmem_limit_bytes=24 * 2**20),
        cost_estimate=pl.CostEstimate(flops=flops, bytes_accessed=size, transcendentals=0),
    )


def selector(owner):
    row, lane = iota((512, 128), 0), iota((512, 128), 1)
    slot = (((row >> 4) & 3) * 2 + ((row >> 1) & 1)) * 8 + (row >> 6)
    hit = (owner == slot) & ((lane & 1) == (row & 1))
    pair = (row >> 2) & 3
    return jnp.concatenate([one_hot(hit & (pair == q)) for q in range(4)], axis=1)


def pack(field, owner):
    wide = jnp.concatenate([field(q) for q in range(4)], axis=1)
    high, low = split(wide)
    chosen = selector(owner)
    return dot_nt(chosen, high) + dot_nt(chosen, low)


def unpack(rows, owner):
    high, low = split(rows)
    chosen = selector(owner)
    return dot_tn(high, chosen) + dot_tn(low, chosen)


def begin_kernel(owner, static_in, packed, work):
    for lon in range(8):
        work[lon] = static_in[pl.ds(lon, 64, stride=8), :]
    packed[...] = pack(lambda q: work[2 * q : 2 * q + 2].reshape(128, 128), owner[...])


def begin_members_kernel(ens_in, perts_in, classes, up, down, ens, perts, flat):
    flat[...] = perts_in[...].astype(f32).reshape(1024, 128)
    for lon in range(8):
        member = ens_in[pl.ds(lon, 64, stride=8), :]
        ens[lon] = member
        perts[lon] = flat[pl.ds(lon, 128, stride=8), :]
        target, place = (down, lon) if lon < 4 else (up, lon - 4)
        target[place * 64 : place * 64 + 64] = member
    marks = classes[...].astype(f32)
    up[256:264] = marks
    down[256:264] = marks


def request_kernel(source_row, column_row, request, ranks):
    source = source_row[...]
    mine = iota((64, 512), 0) == source
    marks = one_hot(mine)
    earlier = one_hot(iota((512, 512), 0) < iota((512, 512), 1))
    count = dot_nn(marks, earlier)
    rank = jnp.sum(jnp.where(mine, count, 0.0), axis=0, keepdims=True).astype(i32)
    ranks[...] = rank
    wanted = column_row[...] + 1
    ranked = one_hot(iota((128, 512), 0) == rank)
    high = jnp.where(mine, (wanted >> 5).astype(f32), 0.0).astype(bf16)
    low = jnp.where(mine, (wanted & 31).astype(f32), 0.0).astype(bf16)
    request[...] = 32.0 * dot_nt(high, ranked) + dot_nt(low, ranked)


def slots_kernel(here, source_row, ranks, weight, innovation, shared, first, second):
    z, level = here[0], here[1]
    source, rank = source_row[...], ranks[...]
    row = iota((256, 512), 0)
    place = ((row >> 7) & 1) * 16 + (row & 15)
    for j, target in enumerate((first, second)):
        for k in range(4):
            target[k * 64 : k * 64 + 64] = shared[k * 128 + 64 : k * 128 + 128]
            target[768 + k * 64 : 832 + k * 64] = shared[k * 128 : k * 128 + 64]
        tile = lax.rem(z + level + 4 * j + 3 * lax.rem(z, 2), 8) * 8 + ((row >> 4) & 7)
        mine = one_hot((source == tile) & (rank == place))
        for kind, values in enumerate((weight, innovation)):
            terms = split(values[...])
            target[256 + kind * 256 : 512 + kind * 256] = dot_nt(mine, terms[0]) + dot_nt(mine, terms[1])


def load_matrices(here, first, second, matrices):
    turn = lax.rem(here[0] - 2 * here[1] + 8, 8)
    for j, part in enumerate((first, second)):
        half = lax.bitwise_xor(lax.div(turn, 4), j)
        for k in range(4):
            block = lax.bitwise_xor(lax.rem(turn, 4), k)
            rows = pl.ds(pl.multiple_of(block * 32, 32), 32)
            for var in range(2):
                start = 768 + k * 64 + var * 32
                matrices[half * 2 + var, rows, :] = part[start : start + 32]


def columns_of(rows):
    blocks = [
        jnp.concatenate([rows[u * 64 + l * 16 : u * 64 + l * 16 + 16] for u in range(8)], axis=0)
        for l in range(4)
    ]
    chunk = iota((128, 128), 1) >> 5
    out = []
    for c in range(4):
        joined = None
        for l in range(4):
            shift = (32 * (l - c)) % 128
            moved = pltpu.roll(blocks[l], shift, 1) if shift else blocks[l]
            joined = moved if l == 0 else jnp.where(chunk == l, moved, joined)
        out.append(joined)
    return out


def store_columns(out, columns, stride, offset):
    chunk = iota((128, 128), 1) >> 5
    for l in range(4):
        joined = None
        for c in range(4):
            shift = (32 * (c - l)) % 128
            moved = pltpu.roll(columns[c], shift, 1) if shift else columns[c]
            joined = moved if c == 0 else jnp.where(chunk == c, moved, joined)
        for u in range(8):
            start = (u * 4 + l) * stride + offset
            out[start : start + 16] = joined[u * 16 : u * 16 + 16]


def choose_half(product):
    half = (iota((256, 128), 0) >> 1) & 1
    return jnp.where(half == 0, product[:, :128], product[:, 128:])


def forward_columns(columns, matrices):
    out = [None] * 4
    for var in range(2):
        stacked = jnp.concatenate([columns[var], columns[2 + var]], axis=0)
        pair = jnp.concatenate([matrices[var], matrices[2 + var]], axis=0)
        chosen = choose_half(three(dot_nt, stacked, pair))
        out[var], out[2 + var] = chosen[:128], chosen[128:]
    return out


def backward_columns(columns, matrices):
    out = [None] * 4
    for var in range(2):
        stacked = jnp.concatenate([columns[var], columns[2 + var]], axis=0)
        pair = jnp.concatenate([matrices[var], matrices[2 + var]], axis=1)
        chosen = choose_half(three(dot_nn, stacked, pair))
        out[var], out[2 + var] = chosen[:128], chosen[128:]
    return out


def first_columns_kernel(here, rows, first, second, state, out, matrices):
    load_matrices(here, first, second, matrices)
    columns = columns_of(rows[...])
    for c in range(4):
        state[c] = columns[c]
    store_columns(out, forward_columns(columns, matrices), 16, 0)


def columns_kernel(last, here, rows, first, second, state, *refs):
    out, matrices = refs[-2], refs[-1]
    load_matrices(here, first, second, matrices)
    pulled = backward_columns(columns_of(rows[...]), matrices)
    columns = [(1.0 - step_length) * state[c] - step_length * pulled[c] for c in range(4)]
    forward = forward_columns(columns, matrices)
    if last:
        store_columns(out, forward, 32, 0)
        store_columns(out, columns, 32, 16)
    else:
        for c in range(4):
            refs[0][c] = columns[c]
        store_columns(out, forward, 16, 0)


def edges_kernel(owner, rows, low, high):
    wide = unpack(rows[...], owner[...])
    for lon in range(8):
        target, place = (low, lon) if lon < 4 else (high, lon - 4)
        q, side = lon // 2, lon % 2
        target[place] = wide[side * 64 : side * 64 + 64, q * 128 : q * 128 + 128]


def last_edges_kernel(owner, rows, low, high, final_static):
    both = rows[...]
    for kind in range(2):
        part = jnp.concatenate([both[p * 32 + kind * 16 : p * 32 + kind * 16 + 16] for p in range(32)], axis=0)
        wide = unpack(part, owner[...])
        for lon in range(8):
            q, side = lon // 2, lon % 2
            value = wide[side * 64 : side * 64 + 64, q * 128 : q * 128 + 128]
            if kind == 0:
                target, place = (low, lon) if lon < 4 else (high, lon - 4)
                target[place] = value
            else:
                final_static[pl.ds(lon, 64, stride=8), :] = value


def weights_kernel(scales, before, own, after, weights, kappa):
    marks = jnp.concatenate([before[...], own[...].astype(f32), after[...]], axis=0)
    lane = iota((16, 128), 1)
    for kind in range(2):
        value = jnp.zeros((24, 128), f32)
        for entry in range(8):
            value = jnp.where(marks == float(entry), scales[kind * 8 + entry], value)
        kappa[kind] = value
        centre = kappa[kind, 4:20]
        east = 0.5 * (centre + kappa[kind, 5:21])
        west = 0.5 * (kappa[kind, 3:19] + centre)
        north = jnp.where(lane < 127, 0.5 * (centre + pltpu.roll(centre, 127, 1)), 0.0)
        south = jnp.where(lane > 0, 0.5 * (centre + pltpu.roll(centre, 1, 1)), 0.0)
        weights[kind, 0] = east
        weights[kind, 1] = west
        weights[kind, 2] = north
        weights[kind, 3] = south
        weights[kind, 4] = 1.0 / (1.0 + east + west + north + south)


def neighbours(field, i, weight):
    return (
        weight(0, i) * field[i + 1]
        + weight(1, i) * field[i - 1]
        + weight(2, i) * pltpu.roll(field[i], 127, 1)
        + weight(3, i) * pltpu.roll(field[i], 1, 1)
    )


def diffuse(source, weight):
    current = dict(enumerate(source))
    for sweep in range(NSWEEP):
        current = {
            i: weight(4, i) * (source[i] + neighbours(current, i, weight))
            for i in range(sweep + 1, 15 - sweep)
        }
    return current


def diffuse_transposed(source, weight):
    carried = dict(enumerate(source))
    total = None
    for sweep in range(NSWEEP):
        scaled = {i: weight(4, i) * carried[i] for i in range(sweep, 16 - sweep)}
        total = {i: scaled[i] if total is None else total[i] + scaled[i] for i in range(4, 12)}
        carried = {i: neighbours(scaled, i, weight) for i in range(sweep + 1, 15 - sweep)}
    return {i: total[i] + carried[i] for i in range(4, 12)}


def weight_of(weights, kind):
    return lambda which, i: weights[kind, which, i : i + 1, :]


def wide_loader(before, low, high, after):
    parts = (before, low, high, after)
    return lambda rows: [parts[i // 4][i % 4, rows, :] for i in range(16)]


def members_kernel(ens, ens_before, ens_after, perts, weights, out):

    def ens_at(rows):
        return (
            [ens_before[pl.ds(i * 64 + rows, 8), :] for i in range(4)]
            + [ens[i, pl.ds(rows, 8), :] for i in range(8)]
            + [ens_after[pl.ds(i * 64 + rows, 8), :] for i in range(4)]
        )

    def levels(step, carry):
        base = pl.multiple_of(step * 8, 8)
        members = [diffuse(ens_at(e * 32 + base), weight_of(weights, 1)) for e in range(2)]
        for var in range(2):
            for lon in range(8):
                total = sum(
                    perts[lon, pl.ds((e * 2 + var) * 32 + base, 8), :] * members[e][lon + 4] for e in range(2)
                )
                out[lon, pl.ds(var * 32 + base, 8), :] = beta_ensemble * total
        return carry

    lax.fori_loop(0, 4, levels, 0)


def increments(loader, members, weights, target):

    def levels(step, carry):
        for var in range(2):
            rows = pl.ds(pl.multiple_of(var * 32 + step * 8, 8), 8)
            smooth = diffuse(loader(rows), weight_of(weights, 0))
            for lon in range(8):
                target[lon, rows, :] = beta_static * smooth[lon + 4] + members[lon, rows, :]
        return carry

    lax.fori_loop(0, 4, levels, 0)


def slot_columns(high, low, start, count, half):
    row = iota((count, 64), 0) + start
    tile = ((row >> 4) & 7) * 8 + (row >> 7)
    repeat = one_hot(tile == iota((count, 64), 1))
    spread = 32.0 * dot_nn(repeat, high) + dot_nn(repeat, low)
    place = (iota((count, 128), 0) & 15) + half * 16
    return jnp.sum(jnp.where(iota((count, 128), 1) == place, spread, 0.0), axis=1, keepdims=True).astype(i32) - 1


def observe_kernel(request, low, high, before, after, members, weights, out, field, terms):
    increments(wide_loader(before, low, high, after), members, weights, field)
    for q in range(4):
        pair = jnp.concatenate([field[2 * q], field[2 * q + 1]], axis=1)
        terms[q] = jnp.concatenate(split(pair), axis=0)
    wanted = request[...].astype(i32)
    first, second = (wanted >> 5).astype(f32).astype(bf16), (wanted & 31).astype(f32).astype(bf16)
    wide = iota((256, 256), 1)

    def block(step, carry):
        start = pl.multiple_of(step * 256, 256)
        sums = []
        for half in range(2):
            column = slot_columns(first, second, start, 256, half)
            total = sum(dot_nt(one_hot(column - q * 256 == wide), terms[q]) for q in range(4))
            sums.append(total + pltpu.roll(total, 64, 1))
        out[pl.ds(start, 256), :] = jnp.where(iota((256, 128), 1) < 64, sums[0], sums[1])
        return carry

    lax.fori_loop(0, 4, block, 0)


def last_kernel(low, high, before, after, members, weights, ens, out, final_ens, field):
    increments(wide_loader(before, low, high, after), members, weights, field)
    for lon in range(8):
        out[pl.ds(lon, 64, stride=8), :] = field[lon]
        final_ens[pl.ds(lon, 64, stride=8), :] = ens[lon]


def operators_kernel(here, arrived, first, second, out, stacked):
    turn = lax.rem(here[0] - 2 * here[1] + 8, 8)
    lane = iota((128, 128), 1) < 64

    def start(u, k, half):
        level = lax.bitwise_xor(lax.rem(turn, 4), k)
        return pl.ds(pl.multiple_of((u * 4 + level) * 32 + half * 16, 16), 16)

    for j, part in enumerate((first, second)):
        half = lax.bitwise_xor(lax.div(turn, 4), j)
        blocks = [
            jnp.concatenate([arrived[start(u, k, half), :] for u in range(8)], axis=0) for k in range(4)
        ]
        operator = part[0:256]
        for pair in range(2):
            even, odd = blocks[2 * pair], blocks[2 * pair + 1]
            lanes = slice(pair * 128, pair * 128 + 128)
            stacked[0:128, lanes] = jnp.where(lane, even, pltpu.roll(odd, 64, 1))
            stacked[128:256, lanes] = jnp.where(lane, pltpu.roll(even, 64, 1), odd)
        observed = three(dot_nn, stacked[...], operator)
        departure = part[256:512] * (observed - part[512:768])
        pulled = three(dot_nt, departure, operator)
        for pair in range(2):
            lanes = slice(pair * 128, pair * 128 + 128)
            upper, lower = pulled[:128, lanes], pulled[128:, lanes]
            values = (
                jnp.where(lane, upper, pltpu.roll(lower, 64, 1)),
                jnp.where(lane, pltpu.roll(upper, 64, 1), lower),
            )
            for side in range(2):
                for u in range(8):
                    out[start(u, 2 * pair + side, half), :] = values[side][u * 16 : u * 16 + 16]


def collect_kernel(request, arrived, perts, low, high, turned, places):
    value = arrived[...]
    first = value.astype(bf16).astype(f32)
    rest = value - first
    lane = iota((1024, 128), 1) < 64
    turned[:, 0:1024] = jnp.where(lane, first, pltpu.roll(rest, 64, 1)).T.astype(bf16)
    turned[:, 1024:2048] = jnp.where(lane, pltpu.roll(first, 64, 1), rest).T.astype(bf16)
    wanted = request[...].astype(i32)
    upper, lower = (wanted >> 5).astype(f32).astype(bf16), (wanted & 31).astype(f32).astype(bf16)
    for half in range(2):
        places[half * 1024 : half * 1024 + 1024] = jnp.broadcast_to(
            slot_columns(upper, lower, 0, 1024, half), (1024, 128)
        )

    def pair(q, carry):
        wide = iota((2048, 128), 1) + q * 256
        hits = jnp.concatenate([one_hot(places[...] == wide), one_hot(places[...] == wide + 128)], axis=1)
        both = dot_nn(turned[...], hits)
        total = both[:64] + both[64:]
        for side in range(2):
            gradient = total[:, side * 128 : side * 128 + 128]
            factor = perts[2 * q + side]
            mixed = [
                factor[e * 64 : e * 64 + 32] * gradient[:32] + factor[e * 64 + 32 : e * 64 + 64] * gradient[32:]
                for e in range(2)
            ]
            value = jnp.concatenate([gradient] + [beta_ensemble * part for part in mixed], axis=0)
            place = lax.rem(q, 2) * 2 + side

            @pl.when(q < 2)
            def _():
                low[place] = value

            @pl.when(q >= 2)
            def _():
                high[place] = value

        return carry

    lax.fori_loop(0, 4, pair, 0)


def pull_kernel(owner, low, high, before, after, weights, packed, field):
    loader = wide_loader(before, low, high, after)

    def levels(step, carry):
        for var in range(2):
            rows = pl.ds(pl.multiple_of(var * 32 + step * 8, 8), 8)
            smooth = diffuse_transposed([beta_static * value for value in loader(rows)], weight_of(weights, 0))
            for lon in range(8):
                field[lon, rows, :] = smooth[lon + 4]
        return carry

    lax.fori_loop(0, 4, levels, 0)
    packed[...] = pack(lambda q: field[2 * q : 2 * q + 2].reshape(128, 128), owner[...])


def pull_members_kernel(low, high, before, after, ens, weights, new_ens, new_low, new_high):
    loader = wide_loader(before, low, high, after)

    def levels(step, carry):
        for e in range(2):
            base = pl.multiple_of(e * 32 + step * 8, 8)
            smooth = diffuse_transposed(loader(pl.ds(64 + base, 8)), weight_of(weights, 1))
            for lon in range(8):
                value = (1.0 - step_length) * ens[lon, pl.ds(base, 8), :] - step_length * smooth[lon + 4]
                new_ens[lon, pl.ds(base, 8), :] = value
                if lon < 4:
                    new_low[pl.ds(lon * 64 + base, 8), :] = value
                else:
                    new_high[pl.ds((lon - 4) * 64 + base, 8), :] = value
        return carry

    lax.fori_loop(0, 4, levels, 0)


def on_device(
    control_static,
    control_ens,
    ens_perts,
    band_sqrt,
    band_owner,
    scale_class,
    static_scales,
    local_scales,
    obs_source,
    obs_column,
    obs_jac,
    innovation,
    obs_weight,
):
    tiles = 64
    upward = [(i, (i + 1) % tiles) for i in range(tiles)]
    downward = [(i, (i - 1) % tiles) for i in range(tiles)]

    def to_plane(value):
        return lax.all_to_all(value, PLANE, 0, 0, tiled=True)

    here = jnp.stack([lax.axis_index("z"), lax.axis_index("yh") * 2 + lax.axis_index("core")]).astype(i32)
    scales = jnp.concatenate([static_scales, local_scales])
    owner = jnp.repeat(band_owner, 2).reshape(1, 128)

    shared = jnp.concatenate(
        [band_sqrt.reshape(64, 128), jnp.transpose(obs_jac, (0, 2, 3, 1)).reshape(64, 128)], axis=0
    )
    swap = [(0, 1), (1, 0)]
    shared = jnp.concatenate([shared, lax.ppermute(shared, "core", swap)], axis=0)
    shared = jnp.concatenate([shared, lax.ppermute(shared, "yh", swap)], axis=0)
    exchange = [
        (z * 4 + l, (z + l + 4 * j + 3 * (z % 2)) % 8 * 4 + z // 2) for j in range(2) for z in range(8) for l in range(4)
    ]

    def spread(value, j):
        return lax.ppermute(value, ("z",) + LEV, exchange[j * 32 : j * 32 + 32])

    (packed,) = call(begin_kernel, [((512, 128), f32)], [((8, 64, 128), f32)], total=2)(
        owner, control_static.reshape(512, 128)
    )
    source_row = obs_source.reshape(1, 512)
    request, ranks = call(request_kernel, [((64, 128), f32), ((1, 512), i32)], total=2)(
        source_row, obs_column.reshape(1, 512)
    )
    parts = call(slots_kernel, [((1024, 128), f32), ((1024, 128), f32)], smem=1, total=6)(
        here, source_row, ranks, obs_weight, innovation, shared
    )
    request, parts, arrived = lax.optimization_barrier((request, parts, to_plane(packed)))
    parts = [spread(parts[j], j) for j in range(2)]
    wanted = lax.all_to_all(request, TILE, 0, 0, tiled=True)
    arrived, wanted, parts, control_ens = lax.optimization_barrier((arrived, wanted, parts, control_ens))

    send_up, send_down, ens, perts = call(
        begin_members_kernel,
        [((264, 128), f32), ((264, 128), f32), ((8, 64, 128), f32), ((8, 128, 128), f32)],
        [((1024, 128), f32)],
        total=3,
    )(control_ens.reshape(512, 128), ens_perts.reshape(128, 8, 128), scale_class)
    from_before = lax.ppermute(send_up, TILE, upward)
    from_after = lax.ppermute(send_down, TILE, downward)
    ens_before, marks_before = from_before[:256], from_before[256:]
    ens_after, marks_after = from_after[:256], from_after[256:]

    state, out = call(
        first_columns_kernel,
        [((4, 128, 128), f32), ((512, 128), f32)],
        [((4, 128, 128), f32)],
        smem=1,
        total=4,
    )(here, arrived, *parts)

    (faces,) = call(weights_kernel, [((2, 5, 16, 128), f32)], [((2, 24, 128), f32)], smem=1, total=4)(
        scales, marks_before, scale_class, marks_after
    )

    half_shape = ((4, 64, 128), f32)
    mixed_shape = ((4, 128, 128), f32)
    scratch = ((8, 64, 128), f32)

    def halos(low, high):
        return lax.ppermute(high, TILE, upward), lax.ppermute(low, TILE, downward)

    def members_of(ens, ens_before, ens_after):
        return call(members_kernel, [((8, 64, 128), f32)], total=5)(ens, ens_before, ens_after, perts, faces)[0]

    for iteration in range(ITERS):
        low, high = call(edges_kernel, [half_shape, half_shape], total=2)(owner, to_plane(out))
        before, after = halos(low, high)
        members = members_of(ens, ens_before, ens_after)
        (outgoing,) = call(
            observe_kernel, [((1024, 128), f32)], [scratch, ((4, 128, 256), bf16)], total=7
        )(wanted, low, high, before, after, members, faces)
        (returned,) = call(operators_kernel, [((1024, 128), f32)], [((256, 256), f32)], smem=1, total=4)(
            here, to_plane(outgoing), *parts
        )
        low, high = call(collect_kernel, [mixed_shape, mixed_shape], [((128, 2048), bf16), ((2048, 128), i32)], total=3)(
            wanted, to_plane(returned), perts
        )
        before, after = halos(low, high)
        (packed,) = call(pull_kernel, [((512, 128), f32)], [scratch], total=6)(owner, low, high, before, after, faces)
        ens, ens_low, ens_high = call(
            pull_members_kernel, [((8, 64, 128), f32), ((256, 128), f32), ((256, 128), f32)], total=6
        )(low, high, before, after, ens, faces)
        ens_before = lax.ppermute(ens_high, TILE, upward)
        ens_after = lax.ppermute(ens_low, TILE, downward)
        last = iteration == ITERS - 1
        results = call(
            functools.partial(columns_kernel, last),
            [((1024, 128), f32)] if last else [((4, 128, 128), f32), ((512, 128), f32)],
            [((4, 128, 128), f32)],
            smem=1,
            total=5,
        )(here, to_plane(packed), *parts, state)
        if not last:
            state = results[0]
        out = results[-1]

    low, high, final_static = call(last_edges_kernel, [half_shape, half_shape, ((512, 128), f32)], total=2)(
        owner, to_plane(out)
    )
    before, after = halos(low, high)
    members = members_of(ens, ens_before, ens_after)
    analysis, final_ens = call(last_kernel, [((512, 128), f32), ((512, 128), f32)], [scratch], total=7)(
        low, high, before, after, members, faces, ens
    )
    return tuple(value.reshape(2, 32, 8, 128) for value in (analysis, final_static, final_ens))


def solution(mesh):
    physical = Mesh(mesh.devices.reshape(8, 2, 4, 2, 2), AXES)
    return jax.shard_map(
        on_device,
        mesh=physical,
        in_specs=(
            P(None, LEV, TILE, None),
            P(None, LEV, TILE, None),
            P(None, None, LEV, TILE, None),
            P(TILE, None, LEV, None),
            P(),
            P(TILE, None),
            P(),
            P(),
            P(TILE, None),
            P(TILE),
            P(TILE, None, None, LEV),
            P(None, TILE),
            P(None, TILE),
        ),
        out_specs=(
            P(None, LEV, TILE, None),
            P(None, LEV, TILE, None),
            P(None, LEV, TILE, None),
        ),
        check_vma=False,
    )
```

```python
import functools

import jax
import jax.numpy as jnp
from jax import lax
from jax.experimental import pallas as pl
from jax.experimental.pallas import tpu as pltpu
from jax.sharding import Mesh, PartitionSpec as P

NSWEEP = 4
ITERS = 2

beta_static = 0.8
beta_ensemble = 0.6
step_length = 0.3

LEV = ("yh", "core")
TILE = ("z", "yl", "x")
PLANE = ("yl", "x", "yh", "core")
AXES = ("z", "yl", "x", "yh", "core")

f32, bf16, i32 = jnp.float32, jnp.bfloat16, jnp.int32


def iota(shape, dim):
    return lax.broadcasted_iota(i32, shape, dim)


def split(value):
    high = value.astype(bf16)
    return high, (value - high.astype(f32)).astype(bf16)


def dot_nn(a, b):
    return lax.dot_general(a, b, (((1,), (0,)), ((), ())), preferred_element_type=f32)


def dot_nt(a, b):
    return lax.dot_general(a, b, (((1,), (1,)), ((), ())), preferred_element_type=f32)


def dot_tn(a, b):
    return lax.dot_general(a, b, (((0,), (0,)), ((), ())), preferred_element_type=f32)


def three(dot, a, b):
    (ah, al), (bh, bl) = split(a), split(b)
    return dot(ah, bh) + (dot(ah, bl) + dot(al, bh))


def one_hot(mask):
    return jnp.where(mask, 1.0, 0.0).astype(bf16)


def call(kernel, outs, scratch=(), smem=0, total=0, flops=10**8, size=6 * 10**6):
    spaces = [pl.BlockSpec(memory_space=pltpu.SMEM)] * smem
    spaces += [pl.BlockSpec(memory_space=pltpu.VMEM)] * (total - smem)
    return pl.pallas_call(
        kernel,
        out_shape=[jax.ShapeDtypeStruct(shape, kind) for shape, kind in outs],
        in_specs=spaces,
        out_specs=[pl.BlockSpec(memory_space=pltpu.VMEM)] * len(outs),
        scratch_shapes=[pltpu.VMEM(shape, kind) for shape, kind in scratch],
        compiler_params=pltpu.CompilerParams(vmem_limit_bytes=24 * 2**20),
        cost_estimate=pl.CostEstimate(flops=flops, bytes_accessed=size, transcendentals=0),
    )


def selector(owner):
    row, lane = iota((512, 128), 0), iota((512, 128), 1)
    slot = (((row >> 4) & 3) * 2 + ((row >> 1) & 1)) * 8 + (row >> 6)
    hit = (owner == slot) & ((lane & 1) == (row & 1))
    pair = (row >> 2) & 3
    return jnp.concatenate([one_hot(hit & (pair == q)) for q in range(4)], axis=1)


def pack(field, owner):
    wide = jnp.concatenate([field(q) for q in range(4)], axis=1)
    high, low = split(wide)
    chosen = selector(owner)
    return dot_nt(chosen, high) + dot_nt(chosen, low)


def unpack(rows, owner):
    high, low = split(rows)
    chosen = selector(owner)
    return dot_tn(high, chosen) + dot_tn(low, chosen)


def begin_kernel(owner, static_in, packed, work):
    for lon in range(8):
        work[lon] = static_in[pl.ds(lon, 64, stride=8), :]
    packed[...] = pack(lambda q: work[2 * q : 2 * q + 2].reshape(128, 128), owner[...])


def begin_members_kernel(ens_in, perts_in, classes, up, down, ens, perts, flat):
    flat[...] = perts_in[...].astype(f32).reshape(1024, 128)
    for lon in range(8):
        member = ens_in[pl.ds(lon, 64, stride=8), :]
        ens[lon] = member
        perts[lon] = flat[pl.ds(lon, 128, stride=8), :]
        target, place = (down, lon) if lon < 4 else (up, lon - 4)
        target[place * 64 : place * 64 + 64] = member
    marks = classes[...].astype(f32)
    up[256:264] = marks
    down[256:264] = marks


def request_kernel(source_row, column_row, request, ranks):
    source = source_row[...]
    mine = iota((64, 512), 0) == source
    marks = one_hot(mine)
    earlier = one_hot(iota((512, 512), 0) < iota((512, 512), 1))
    count = dot_nn(marks, earlier)
    rank = jnp.sum(jnp.where(mine, count, 0.0), axis=0, keepdims=True).astype(i32)
    ranks[...] = rank
    wanted = column_row[...] + 1
    ranked = one_hot(iota((128, 512), 0) == rank)
    high = jnp.where(mine, (wanted >> 5).astype(f32), 0.0).astype(bf16)
    low = jnp.where(mine, (wanted & 31).astype(f32), 0.0).astype(bf16)
    request[...] = 32.0 * dot_nt(high, ranked) + dot_nt(low, ranked)


def slots_kernel(here, source_row, ranks, weight, innovation, shared, first, second):
    z, level = here[0], here[1]
    source, rank = source_row[...], ranks[...]
    row = iota((256, 512), 0)
    place = ((row >> 7) & 1) * 16 + (row & 15)
    for j, target in enumerate((first, second)):
        for k in range(4):
            target[k * 64 : k * 64 + 64] = shared[k * 128 + 64 : k * 128 + 128]
            target[768 + k * 64 : 832 + k * 64] = shared[k * 128 : k * 128 + 64]
        tile = lax.rem(z + level + 4 * j + 3 * lax.rem(z, 2), 8) * 8 + ((row >> 4) & 7)
        mine = one_hot((source == tile) & (rank == place))
        for kind, values in enumerate((weight, innovation)):
            terms = split(values[...])
            target[256 + kind * 256 : 512 + kind * 256] = dot_nt(mine, terms[0]) + dot_nt(mine, terms[1])


def load_matrices(here, first, second, matrices):
    turn = lax.rem(here[0] - 2 * here[1] + 8, 8)
    for j, part in enumerate((first, second)):
        half = lax.bitwise_xor(lax.div(turn, 4), j)
        for k in range(4):
            block = lax.bitwise_xor(lax.rem(turn, 4), k)
            rows = pl.ds(pl.multiple_of(block * 32, 32), 32)
            for var in range(2):
                start = 768 + k * 64 + var * 32
                matrices[half * 2 + var, rows, :] = part[start : start + 32]


def columns_of(rows):
    blocks = [
        jnp.concatenate([rows[u * 64 + l * 16 : u * 64 + l * 16 + 16] for u in range(8)], axis=0)
        for l in range(4)
    ]
    chunk = iota((128, 128), 1) >> 5
    out = []
    for c in range(4):
        joined = None
        for l in range(4):
            shift = (32 * (l - c)) % 128
            moved = pltpu.roll(blocks[l], shift, 1) if shift else blocks[l]
            joined = moved if l == 0 else jnp.where(chunk == l, moved, joined)
        out.append(joined)
    return out


def store_columns(out, columns, stride, offset):
    chunk = iota((128, 128), 1) >> 5
    for l in range(4):
        joined = None
        for c in range(4):
            shift = (32 * (c - l)) % 128
            moved = pltpu.roll(columns[c], shift, 1) if shift else columns[c]
            joined = moved if c == 0 else jnp.where(chunk == c, moved, joined)
        for u in range(8):
            start = (u * 4 + l) * stride + offset
            out[start : start + 16] = joined[u * 16 : u * 16 + 16]


def choose_half(product):
    half = (iota((256, 128), 0) >> 1) & 1
    return jnp.where(half == 0, product[:, :128], product[:, 128:])


def forward_columns(columns, matrices):
    out = [None] * 4
    for var in range(2):
        stacked = jnp.concatenate([columns[var], columns[2 + var]], axis=0)
        pair = jnp.concatenate([matrices[var], matrices[2 + var]], axis=0)
        chosen = choose_half(three(dot_nt, stacked, pair))
        out[var], out[2 + var] = chosen[:128], chosen[128:]
    return out


def backward_columns(columns, matrices):
    out = [None] * 4
    for var in range(2):
        stacked = jnp.concatenate([columns[var], columns[2 + var]], axis=0)
        pair = jnp.concatenate([matrices[var], matrices[2 + var]], axis=1)
        chosen = choose_half(three(dot_nn, stacked, pair))
        out[var], out[2 + var] = chosen[:128], chosen[128:]
    return out


def first_columns_kernel(here, rows, first, second, state, out, matrices):
    load_matrices(here, first, second, matrices)
    columns = columns_of(rows[...])
    for c in range(4):
        state[c] = columns[c]
    store_columns(out, forward_columns(columns, matrices), 16, 0)


def columns_kernel(last, here, rows, first, second, state, *refs):
    out, matrices = refs[-2], refs[-1]
    load_matrices(here, first, second, matrices)
    pulled = backward_columns(columns_of(rows[...]), matrices)
    columns = [(1.0 - step_length) * state[c] - step_length * pulled[c] for c in range(4)]
    forward = forward_columns(columns, matrices)
    if last:
        store_columns(out, forward, 32, 0)
        store_columns(out, columns, 32, 16)
    else:
        for c in range(4):
            refs[0][c] = columns[c]
        store_columns(out, forward, 16, 0)


def edges_kernel(owner, rows, low, high):
    wide = unpack(rows[...], owner[...])
    for lon in range(8):
        target, place = (low, lon) if lon < 4 else (high, lon - 4)
        q, side = lon // 2, lon % 2
        target[place] = wide[side * 64 : side * 64 + 64, q * 128 : q * 128 + 128]


def last_edges_kernel(owner, rows, low, high, final_static):
    both = rows[...]
    for kind in range(2):
        part = jnp.concatenate([both[p * 32 + kind * 16 : p * 32 + kind * 16 + 16] for p in range(32)], axis=0)
        wide = unpack(part, owner[...])
        for lon in range(8):
            q, side = lon // 2, lon % 2
            value = wide[side * 64 : side * 64 + 64, q * 128 : q * 128 + 128]
            if kind == 0:
                target, place = (low, lon) if lon < 4 else (high, lon - 4)
                target[place] = value
            else:
                final_static[pl.ds(lon, 64, stride=8), :] = value


def weights_kernel(scales, before, own, after, weights, kappa):
    marks = jnp.concatenate([before[...], own[...].astype(f32), after[...]], axis=0)
    lane = iota((16, 128), 1)
    for kind in range(2):
        value = jnp.zeros((24, 128), f32)
        for entry in range(8):
            value = jnp.where(marks == float(entry), scales[kind * 8 + entry], value)
        kappa[kind] = value
        centre = kappa[kind, 4:20]
        east = 0.5 * (centre + kappa[kind, 5:21])
        west = 0.5 * (kappa[kind, 3:19] + centre)
        north = jnp.where(lane < 127, 0.5 * (centre + pltpu.roll(centre, 127, 1)), 0.0)
        south = jnp.where(lane > 0, 0.5 * (centre + pltpu.roll(centre, 1, 1)), 0.0)
        weights[kind, 0] = east
        weights[kind, 1] = west
        weights[kind, 2] = north
        weights[kind, 3] = south
        weights[kind, 4] = 1.0 / (1.0 + east + west + north + south)


def neighbours(field, i, weight):
    return (
        weight(0, i) * field[i + 1]
        + weight(1, i) * field[i - 1]
        + weight(2, i) * pltpu.roll(field[i], 127, 1)
        + weight(3, i) * pltpu.roll(field[i], 1, 1)
    )


def diffuse(source, weight):
    current = dict(enumerate(source))
    for sweep in range(NSWEEP):
        current = {
            i: weight(4, i) * (source[i] + neighbours(current, i, weight))
            for i in range(sweep + 1, 15 - sweep)
        }
    return current


def diffuse_transposed(source, weight):
    carried = dict(enumerate(source))
    total = None
    for sweep in range(NSWEEP):
        scaled = {i: weight(4, i) * carried[i] for i in range(sweep, 16 - sweep)}
        total = {i: scaled[i] if total is None else total[i] + scaled[i] for i in range(4, 12)}
        carried = {i: neighbours(scaled, i, weight) for i in range(sweep + 1, 15 - sweep)}
    return {i: total[i] + carried[i] for i in range(4, 12)}


def weight_of(weights, kind):
    return lambda which, i: weights[kind, which, i : i + 1, :]


def wide_loader(before, low, high, after):
    parts = (before, low, high, after)
    return lambda rows: [parts[i // 4][i % 4, rows, :] for i in range(16)]


def members_kernel(ens, ens_before, ens_after, perts, weights, out):

    def ens_at(rows):
        return (
            [ens_before[pl.ds(i * 64 + rows, 8), :] for i in range(4)]
            + [ens[i, pl.ds(rows, 8), :] for i in range(8)]
            + [ens_after[pl.ds(i * 64 + rows, 8), :] for i in range(4)]
        )

    def levels(step, carry):
        base = pl.multiple_of(step * 8, 8)
        members = [diffuse(ens_at(e * 32 + base), weight_of(weights, 1)) for e in range(2)]
        for var in range(2):
            for lon in range(8):
                total = sum(
                    perts[lon, pl.ds((e * 2 + var) * 32 + base, 8), :] * members[e][lon + 4] for e in range(2)
                )
                out[lon, pl.ds(var * 32 + base, 8), :] = beta_ensemble * total
        return carry

    lax.fori_loop(0, 4, levels, 0)


def increments(loader, members, weights, target):

    def levels(step, carry):
        for var in range(2):
            rows = pl.ds(pl.multiple_of(var * 32 + step * 8, 8), 8)
            smooth = diffuse(loader(rows), weight_of(weights, 0))
            for lon in range(8):
                target[lon, rows, :] = beta_static * smooth[lon + 4] + members[lon, rows, :]
        return carry

    lax.fori_loop(0, 4, levels, 0)


def slot_columns(high, low, start, count, half):
    row = iota((count, 64), 0) + start
    tile = ((row >> 4) & 7) * 8 + (row >> 7)
    repeat = one_hot(tile == iota((count, 64), 1))
    spread = 32.0 * dot_nn(repeat, high) + dot_nn(repeat, low)
    place = (iota((count, 128), 0) & 15) + half * 16
    return jnp.sum(jnp.where(iota((count, 128), 1) == place, spread, 0.0), axis=1, keepdims=True).astype(i32) - 1


def observe_kernel(request, low, high, before, after, members, weights, out, field, terms):
    increments(wide_loader(before, low, high, after), members, weights, field)
    for q in range(4):
        pair = jnp.concatenate([field[2 * q], field[2 * q + 1]], axis=1)
        terms[q] = jnp.concatenate(split(pair), axis=0)
    wanted = request[...].astype(i32)
    first, second = (wanted >> 5).astype(f32).astype(bf16), (wanted & 31).astype(f32).astype(bf16)
    wide = iota((512, 256), 1)

    def block(step, carry):
        start = pl.multiple_of(step * 512, 512)
        sums = []
        for half in range(2):
            column = slot_columns(first, second, start, 512, half)
            total = sum(dot_nt(one_hot(column - q * 256 == wide), terms[q]) for q in range(4))
            sums.append(total + pltpu.roll(total, 64, 1))
        out[pl.ds(start, 512), :] = jnp.where(iota((512, 128), 1) < 64, sums[0], sums[1])
        return carry

    lax.fori_loop(0, 2, block, 0)


def last_kernel(low, high, before, after, members, weights, ens, out, final_ens, field):
    increments(wide_loader(before, low, high, after), members, weights, field)
    for lon in range(8):
        out[pl.ds(lon, 64, stride=8), :] = field[lon]
        final_ens[pl.ds(lon, 64, stride=8), :] = ens[lon]


def operators_kernel(here, arrived, first, second, out, stacked):
    turn = lax.rem(here[0] - 2 * here[1] + 8, 8)
    lane = iota((128, 128), 1) < 64

    def start(u, k, half):
        level = lax.bitwise_xor(lax.rem(turn, 4), k)
        return pl.ds(pl.multiple_of((u * 4 + level) * 32 + half * 16, 16), 16)

    for j, part in enumerate((first, second)):
        half = lax.bitwise_xor(lax.div(turn, 4), j)
        blocks = [
            jnp.concatenate([arrived[start(u, k, half), :] for u in range(8)], axis=0) for k in range(4)
        ]
        operator = part[0:256]
        for pair in range(2):
            even, odd = blocks[2 * pair], blocks[2 * pair + 1]
            lanes = slice(pair * 128, pair * 128 + 128)
            stacked[0:128, lanes] = jnp.where(lane, even, pltpu.roll(odd, 64, 1))
            stacked[128:256, lanes] = jnp.where(lane, pltpu.roll(even, 64, 1), odd)
        observed = three(dot_nn, stacked[...], operator)
        departure = part[256:512] * (observed - part[512:768])
        pulled = three(dot_nt, departure, operator)
        for pair in range(2):
            lanes = slice(pair * 128, pair * 128 + 128)
            upper, lower = pulled[:128, lanes], pulled[128:, lanes]
            values = (
                jnp.where(lane, upper, pltpu.roll(lower, 64, 1)),
                jnp.where(lane, pltpu.roll(upper, 64, 1), lower),
            )
            for side in range(2):
                for u in range(8):
                    out[start(u, 2 * pair + side, half), :] = values[side][u * 16 : u * 16 + 16]


def collect_kernel(request, arrived, perts, low, high, turned, places):
    value = arrived[...]
    first = value.astype(bf16).astype(f32)
    rest = value - first
    lane = iota((1024, 128), 1) < 64
    turned[:, 0:1024] = jnp.where(lane, first, pltpu.roll(rest, 64, 1)).T.astype(bf16)
    turned[:, 1024:2048] = jnp.where(lane, pltpu.roll(first, 64, 1), rest).T.astype(bf16)
    wanted = request[...].astype(i32)
    upper, lower = (wanted >> 5).astype(f32).astype(bf16), (wanted & 31).astype(f32).astype(bf16)
    for half in range(2):
        places[half * 1024 : half * 1024 + 1024] = jnp.broadcast_to(
            slot_columns(upper, lower, 0, 1024, half), (1024, 128)
        )

    def pair(q, carry):
        wide = iota((2048, 128), 1) + q * 256
        hits = jnp.concatenate([one_hot(places[...] == wide), one_hot(places[...] == wide + 128)], axis=1)
        both = dot_nn(turned[...], hits)
        total = both[:64] + both[64:]
        for side in range(2):
            gradient = total[:, side * 128 : side * 128 + 128]
            factor = perts[2 * q + side]
            mixed = [
                factor[e * 64 : e * 64 + 32] * gradient[:32] + factor[e * 64 + 32 : e * 64 + 64] * gradient[32:]
                for e in range(2)
            ]
            value = jnp.concatenate([gradient] + [beta_ensemble * part for part in mixed], axis=0)
            place = lax.rem(q, 2) * 2 + side

            @pl.when(q < 2)
            def _():
                low[place] = value

            @pl.when(q >= 2)
            def _():
                high[place] = value

        return carry

    lax.fori_loop(0, 4, pair, 0)


def pull_kernel(owner, low, high, before, after, weights, packed, field):
    loader = wide_loader(before, low, high, after)

    def levels(step, carry):
        for var in range(2):
            rows = pl.ds(pl.multiple_of(var * 32 + step * 8, 8), 8)
            smooth = diffuse_transposed([beta_static * value for value in loader(rows)], weight_of(weights, 0))
            for lon in range(8):
                field[lon, rows, :] = smooth[lon + 4]
        return carry

    lax.fori_loop(0, 4, levels, 0)
    packed[...] = pack(lambda q: field[2 * q : 2 * q + 2].reshape(128, 128), owner[...])


def pull_members_kernel(low, high, before, after, ens, weights, new_ens, new_low, new_high):
    loader = wide_loader(before, low, high, after)

    def levels(step, carry):
        for e in range(2):
            base = pl.multiple_of(e * 32 + step * 8, 8)
            smooth = diffuse_transposed(loader(pl.ds(64 + base, 8)), weight_of(weights, 1))
            for lon in range(8):
                value = (1.0 - step_length) * ens[lon, pl.ds(base, 8), :] - step_length * smooth[lon + 4]
                new_ens[lon, pl.ds(base, 8), :] = value
                if lon < 4:
                    new_low[pl.ds(lon * 64 + base, 8), :] = value
                else:
                    new_high[pl.ds((lon - 4) * 64 + base, 8), :] = value
        return carry

    lax.fori_loop(0, 4, levels, 0)


def on_device(
    control_static,
    control_ens,
    ens_perts,
    band_sqrt,
    band_owner,
    scale_class,
    static_scales,
    local_scales,
    obs_source,
    obs_column,
    obs_jac,
    innovation,
    obs_weight,
):
    tiles = 64
    upward = [(i, (i + 1) % tiles) for i in range(tiles)]
    downward = [(i, (i - 1) % tiles) for i in range(tiles)]

    def to_plane(value):
        return lax.all_to_all(value, PLANE, 0, 0, tiled=True)

    here = jnp.stack([lax.axis_index("z"), lax.axis_index("yh") * 2 + lax.axis_index("core")]).astype(i32)
    scales = jnp.concatenate([static_scales, local_scales])
    owner = jnp.repeat(band_owner, 2).reshape(1, 128)

    shared = jnp.concatenate(
        [band_sqrt.reshape(64, 128), jnp.transpose(obs_jac, (0, 2, 3, 1)).reshape(64, 128)], axis=0
    )
    swap = [(0, 1), (1, 0)]
    shared = jnp.concatenate([shared, lax.ppermute(shared, "core", swap)], axis=0)
    shared = jnp.concatenate([shared, lax.ppermute(shared, "yh", swap)], axis=0)
    exchange = [
        (z * 4 + l, (z + l + 4 * j + 3 * (z % 2)) % 8 * 4 + z // 2) for j in range(2) for z in range(8) for l in range(4)
    ]

    def spread(value, j):
        return lax.ppermute(value, ("z",) + LEV, exchange[j * 32 : j * 32 + 32])

    (packed,) = call(begin_kernel, [((512, 128), f32)], [((8, 64, 128), f32)], total=2)(
        owner, control_static.reshape(512, 128)
    )
    source_row = obs_source.reshape(1, 512)
    request, ranks = call(request_kernel, [((64, 128), f32), ((1, 512), i32)], total=2)(
        source_row, obs_column.reshape(1, 512)
    )
    parts = call(slots_kernel, [((1024, 128), f32), ((1024, 128), f32)], smem=1, total=6)(
        here, source_row, ranks, obs_weight, innovation, shared
    )
    request, parts, arrived = lax.optimization_barrier((request, parts, to_plane(packed)))
    parts = [spread(parts[j], j) for j in range(2)]
    wanted = lax.all_to_all(request, TILE, 0, 0, tiled=True)
    arrived, wanted, parts, control_ens = lax.optimization_barrier((arrived, wanted, parts, control_ens))

    send_up, send_down, ens, perts = call(
        begin_members_kernel,
        [((264, 128), f32), ((264, 128), f32), ((8, 64, 128), f32), ((8, 128, 128), f32)],
        [((1024, 128), f32)],
        total=3,
    )(control_ens.reshape(512, 128), ens_perts.reshape(128, 8, 128), scale_class)
    from_before = lax.ppermute(send_up, TILE, upward)
    from_after = lax.ppermute(send_down, TILE, downward)
    ens_before, marks_before = from_before[:256], from_before[256:]
    ens_after, marks_after = from_after[:256], from_after[256:]

    state, out = call(
        first_columns_kernel,
        [((4, 128, 128), f32), ((512, 128), f32)],
        [((4, 128, 128), f32)],
        smem=1,
        total=4,
    )(here, arrived, *parts)

    (faces,) = call(weights_kernel, [((2, 5, 16, 128), f32)], [((2, 24, 128), f32)], smem=1, total=4)(
        scales, marks_before, scale_class, marks_after
    )

    half_shape = ((4, 64, 128), f32)
    mixed_shape = ((4, 128, 128), f32)
    scratch = ((8, 64, 128), f32)

    def halos(low, high):
        return lax.ppermute(high, TILE, upward), lax.ppermute(low, TILE, downward)

    def members_of(ens, ens_before, ens_after):
        return call(members_kernel, [((8, 64, 128), f32)], total=5)(ens, ens_before, ens_after, perts, faces)[0]

    for iteration in range(ITERS):
        low, high = call(edges_kernel, [half_shape, half_shape], total=2)(owner, to_plane(out))
        before, after = halos(low, high)
        members = members_of(ens, ens_before, ens_after)
        (outgoing,) = call(
            observe_kernel, [((1024, 128), f32)], [scratch, ((4, 128, 256), bf16)], total=7
        )(wanted, low, high, before, after, members, faces)
        (returned,) = call(operators_kernel, [((1024, 128), f32)], [((256, 256), f32)], smem=1, total=4)(
            here, to_plane(outgoing), *parts
        )
        low, high = call(collect_kernel, [mixed_shape, mixed_shape], [((128, 2048), bf16), ((2048, 128), i32)], total=3)(
            wanted, to_plane(returned), perts
        )
        before, after = halos(low, high)
        (packed,) = call(pull_kernel, [((512, 128), f32)], [scratch], total=6)(owner, low, high, before, after, faces)
        ens, ens_low, ens_high = call(
            pull_members_kernel, [((8, 64, 128), f32), ((256, 128), f32), ((256, 128), f32)], total=6
        )(low, high, before, after, ens, faces)
        ens_before = lax.ppermute(ens_high, TILE, upward)
        ens_after = lax.ppermute(ens_low, TILE, downward)
        last = iteration == ITERS - 1
        results = call(
            functools.partial(columns_kernel, last),
            [((1024, 128), f32)] if last else [((4, 128, 128), f32), ((512, 128), f32)],
            [((4, 128, 128), f32)],
            smem=1,
            total=5,
        )(here, to_plane(packed), *parts, state)
        if not last:
            state = results[0]
        out = results[-1]

    low, high, final_static = call(last_edges_kernel, [half_shape, half_shape, ((512, 128), f32)], total=2)(
        owner, to_plane(out)
    )
    before, after = halos(low, high)
    members = members_of(ens, ens_before, ens_after)
    analysis, final_ens = call(last_kernel, [((512, 128), f32), ((512, 128), f32)], [scratch], total=7)(
        low, high, before, after, members, faces, ens
    )
    return tuple(value.reshape(2, 32, 8, 128) for value in (analysis, final_static, final_ens))


def solution(mesh):
    physical = Mesh(mesh.devices.reshape(8, 2, 4, 2, 2), AXES)
    return jax.shard_map(
        on_device,
        mesh=physical,
        in_specs=(
            P(None, LEV, TILE, None),
            P(None, LEV, TILE, None),
            P(None, None, LEV, TILE, None),
            P(TILE, None, LEV, None),
            P(),
            P(TILE, None),
            P(),
            P(),
            P(TILE, None),
            P(TILE),
            P(TILE, None, None, LEV),
            P(None, TILE),
            P(None, TILE),
        ),
        out_specs=(
            P(None, LEV, TILE, None),
            P(None, LEV, TILE, None),
            P(None, LEV, TILE, None),
        ),
        check_vma=False,
    )
```
